256 devices in a mesh: freq: 8 (over z), bl: 32 (over y, x, core).
Axes of the slice: x: 4, y: 4, z: 8, core: 2. Of those that a mesh axis runs over, the one named last changes fastest.
Arguments:
- vis: float32 [2, 256, 65536], P(None, 'freq', 'bl'), may hold values from -60 to 60
- coherency: bfloat16 [2, 4, 256, 65536], P(None, None, 'freq', 'bl'), may hold values from -6 to 6
- gains_init: float32 [2, 4, 256, 512], P(None, None, 'freq', 'bl'), may hold values from -4 to 4
- station_pairs: int32 [2, 65536], P(None, 'bl'), may hold values from 0 to 511, as said below
Outputs:
- gains: float32 [2, 4, 256, 512], P(None, None, 'freq', 'bl')
- consensus: float32 [2, 4, 256, 512], P(None, None, 'freq', 'bl')
The draws below stay inside these ranges and needn't reach their ends.
Inputs may be any that keep to these rules, and one draw needn't show every extreme that they name: `station_pairs`: in each column the two stations differ.
All inputs are finite; a program needn't handle non-finite values.
Results may differ from the reference program's by a relative error of at most 0.0013.
Values may be sent and summed in bfloat16 or wider, within the bound.
No kernel may reach another device: no remote copies, remote signals or barrier semaphores. Data moves between devices by JAX's collectives and lax.ppermute only.
A program may use at most 64 MiB of HBM per device.

```python
import math
import jax
import jax.numpy as jnp
from jax import lax

STATION_TOTAL = 512
SKY_DIRECTIONS = 4
CHANNELS_LOCAL = 32
ITERS = 2
ROUNDS = 2
CHANNEL_TOTAL = 256
BASELINE_TOTAL = 65536


def pair_draw(key):
    folded_key = jax.random.fold_in(key, 101)
    first_station_key, offset_key = jax.random.split(folded_key)
    first_station = jax.random.randint(first_station_key, (BASELINE_TOTAL,), 0, STATION_TOTAL, dtype=jnp.int32)
    offset_sample = jax.random.randint(offset_key, (BASELINE_TOTAL,), 1, STATION_TOTAL, dtype=jnp.int32)
    second = (first_station + offset_sample) % STATION_TOTAL
    first_station = first_station.at[0].set(0)
    second = second.at[0].set(STATION_TOTAL - 1)
    return jnp.stack([first_station, second]).astype(jnp.int32)


def coherency_draw(key):
    folded_key = jax.random.fold_in(key, 102)
    value_rows = jax.random.normal(folded_key, (2, SKY_DIRECTIONS, CHANNEL_TOTAL, BASELINE_TOTAL), dtype=jnp.float32)
    return jnp.clip(value_rows, -6.0, 6.0)


def draw_station_pairs(key, part):
    return pair_draw(key)


def draw_coherency(key, part):
    return coherency_draw(key).astype(jnp.bfloat16)


def draw_vis(key, part):
    pairs = pair_draw(key)
    coh = coherency_draw(key).astype(jnp.bfloat16).astype(jnp.float32)
    folded_key = jax.random.fold_in(key, 103)
    key_amp, key_phase, key_wobble, noise_key = jax.random.split(folded_key, 4)
    amplitude = 1.0 + 0.2 * jnp.clip(jax.random.normal(key_amp, (SKY_DIRECTIONS, CHANNEL_TOTAL, STATION_TOTAL), dtype=jnp.float32), -3.0, 3.0)
    phase = jax.random.uniform(key_phase, (SKY_DIRECTIONS, 1, STATION_TOTAL), minval=-math.pi, maxval=math.pi, dtype=jnp.float32)
    phase = phase + 0.3 * jnp.clip(jax.random.normal(key_wobble, (SKY_DIRECTIONS, CHANNEL_TOTAL, STATION_TOTAL), dtype=jnp.float32), -3.0, 3.0)
    true_re = amplitude * jnp.cos(phase)
    true_im = amplitude * jnp.sin(phase)
    near_re = jnp.take(true_re, pairs[0], axis=2)
    near_im = jnp.take(true_im, pairs[0], axis=2)
    far_re = jnp.take(true_re, pairs[1], axis=2)
    far_im = jnp.take(true_im, pairs[1], axis=2)
    z_re = coh[0] * far_re + coh[1] * far_im
    z_im = coh[1] * far_re - coh[0] * far_im
    model_re = jnp.sum(near_re * z_re - near_im * z_im, axis=0)
    model_im = jnp.sum(near_re * z_im + near_im * z_re, axis=0)
    noise_sample = 0.3 * jnp.clip(jax.random.normal(noise_key, (2, CHANNEL_TOTAL, BASELINE_TOTAL), dtype=jnp.float32), -4.0, 4.0)
    return jnp.clip(jnp.stack([model_re, model_im]) + noise_sample, -60.0, 60.0)


def steps_of(own_key, dims, pieces, smallest, top_value):
    def one(dim, shards_of):
        steps = jax.random.uniform(jax.random.fold_in(jax.random.fold_in(own_key, 6), dim), (shards_of,), jnp.float32, smallest / len(pieces), top_value / len(pieces))
        return jnp.repeat(jnp.exp(steps), dims[dim] // shards_of).reshape((-1,) + (1,) * (len(dims) - dim - 1))

    loudness = one(*pieces[0])
    for cut in pieces[1:]:
        loudness = loudness * one(*cut)
    return loudness


def scatter_about(rng, extent, width, limit, shards=(), held_as=jnp.bfloat16):
    entries = jax.random.normal(rng, extent, jnp.float32) * width
    if len(shards) > 0:
        entries = steps_of(rng, extent, shards, -0.22, 0.18) * entries
    return jnp.clip(entries, min=-limit, max=limit).astype(held_as)


def setup_inputs(seed: int = 0) -> dict:
    splits = jax.random.split(jax.random.key(seed), 5)
    vis = draw_vis(jax.random.fold_in(splits[4], 71), 0)
    coherency = draw_coherency(jax.random.fold_in(splits[4], 71), 0)
    gains_init = scatter_about(splits[2], (2, SKY_DIRECTIONS, CHANNEL_TOTAL, STATION_TOTAL), 0.7, 4.0, ((2, 8), (3, 32)), jnp.float32)
    station_pairs = draw_station_pairs(jax.random.fold_in(splits[4], 71), 0)
    return {"vis": vis, "coherency": coherency, "gains_init": gains_init, "station_pairs": station_pairs}


def basis_rows(channels):
    position = (2.0 * jnp.arange(channels, dtype=jnp.float32) + 1.0) / channels - 1.0
    raw = [jnp.ones_like(position), position, position * position, position * position * position]
    rows = []
    for vector in raw:
        for other in rows:
            vector = vector - jnp.sum(other * vector) * other
        rows.append(vector / jnp.sqrt(jnp.sum(vector * vector)))
    return jnp.stack(rows)

def model_terms(vis, coherency, near, far):
    coh_re = coherency[0].astype(jnp.float32)
    coh_im = coherency[1].astype(jnp.float32)
    z_re = coh_re * far[0] + coh_im * far[1]
    z_im = coh_im * far[0] - coh_re * far[1]
    x_re = near[0] * coh_re - near[1] * coh_im
    x_im = near[0] * coh_im + near[1] * coh_re
    model_re = lax.optimization_barrier(jnp.sum(near[0] * z_re - near[1] * z_im, axis=0))
    model_im = lax.optimization_barrier(jnp.sum(near[0] * z_im + near[1] * z_re, axis=0))
    res_re = (vis[0] - model_re)[None]
    res_im = (vis[1] - model_im)[None]
    first_terms = jnp.stack([res_re * z_re + res_im * z_im, res_im * z_re - res_re * z_im, z_re * z_re + z_im * z_im]).astype(jnp.bfloat16)
    second_terms = jnp.stack([res_re * x_re + res_im * x_im, res_re * x_im - res_im * x_re, x_re * x_re + x_im * x_im]).astype(jnp.bfloat16)
    return (first_terms, second_terms)

def advance(gains, sums, target, penalty_weight):
    return gains + (sums[0:2] + penalty_weight * (target - gains)) / (2.0 * sums[2] + penalty_weight)

def station_total(terms, index):
    moved = jnp.moveaxis(terms.astype(jnp.float32), 3, 0)
    summed = jax.ops.segment_sum(moved, index, num_segments=STATION_TOTAL)
    return jnp.moveaxis(summed, 0, 3)

def reference(vis, coherency, gains_init, station_pairs):
    basis = basis_rows(CHANNEL_TOTAL)
    penalty_weight = 2.0 * BASELINE_TOTAL / STATION_TOTAL
    first_index = station_pairs[0]
    second_index = station_pairs[1]
    block_list = CHANNEL_TOTAL // CHANNELS_LOCAL
    visibility_blocks = jnp.moveaxis(vis.reshape(2, block_list, CHANNELS_LOCAL, BASELINE_TOTAL), 1, 0)
    coherency_blocks = jnp.moveaxis(coherency.reshape(2, SKY_DIRECTIONS, block_list, CHANNELS_LOCAL, BASELINE_TOTAL), 2, 0)

    def one_block(items):
        vis_part, coh_part, gain_part, target_part = items
        rounded = lax.optimization_barrier(gain_part.astype(jnp.bfloat16)).astype(jnp.float32)
        near = jnp.take(rounded, first_index, axis=3)
        far = jnp.take(rounded, second_index, axis=3)
        first_terms, second_terms = model_terms(vis_part, coh_part, near, far)
        sums = station_total(first_terms, first_index) + station_total(second_terms, second_index)
        return advance(gain_part, sums, target_part, penalty_weight)

    def sweep(gains, target):
        gain_blocks = jnp.moveaxis(gains.reshape(2, SKY_DIRECTIONS, block_list, CHANNELS_LOCAL, STATION_TOTAL), 2, 0)
        target_blocks = jnp.moveaxis(target.reshape(2, SKY_DIRECTIONS, block_list, CHANNELS_LOCAL, STATION_TOTAL), 2, 0)
        result = lax.map(one_block, (visibility_blocks, coherency_blocks, gain_blocks, target_blocks))
        return jnp.moveaxis(result, 0, 2).reshape(2, SKY_DIRECTIONS, CHANNEL_TOTAL, STATION_TOTAL)
    gains = gains_init
    target = gains_init
    dual = jnp.zeros_like(gains_init)
    consensus = gains_init
    for round_index in range(ROUNDS):
        for step_index in range(ITERS):
            gains = sweep(gains, target)
        blend = gains + dual
        coefficients = jnp.einsum('jk,adks->jads', basis, blend, precision=lax.Precision.HIGHEST)
        consensus = jnp.einsum('jk,jads->adks', basis, coefficients, precision=lax.Precision.HIGHEST)
        dual = dual + gains - consensus
        target = consensus - dual
    return (gains, consensus)
```

```python
import functools

import jax
import jax.numpy as jnp
import numpy as np
from jax import lax
from jax.experimental import pallas as pl
from jax.experimental.pallas import tpu as pltpu
from jax.sharding import Mesh, PartitionSpec as P

STATION_TOTAL = 512
SKY_DIRECTIONS = 4
ITERS = 2
ROUNDS = 2
LANES = 128
PARTS = STATION_TOTAL // LANES
CHUNK = 2048
f32, bf16, i32 = jnp.float32, jnp.bfloat16, jnp.int32


def basis_rows(channels):
    position = (2.0 * np.arange(channels) + 1.0) / channels - 1.0
    rows = []
    for vector in [np.ones_like(position), position, position**2, position**3]:
        for other in rows:
            vector = vector - np.sum(other * vector) * other
        rows.append(vector / np.sqrt(np.sum(vector * vector)))
    return np.stack(rows).astype(np.float32)


def lookup(parts, low, bits):
    picked = [jnp.take_along_axis(p, low, axis=1, mode="promise_in_bounds") for p in parts]
    return jnp.where(
        bits[1], jnp.where(bits[0], picked[3], picked[2]), jnp.where(bits[0], picked[1], picked[0])
    )


def column_terms(coh_re, coh_im, misc, parts_re, parts_im, sublane):
    def station(row):
        index = jnp.broadcast_to((misc[row : row + 1] + 256.0).astype(i32), (8, LANES))
        return index & (LANES - 1), index >> 7

    low_first, high_first = station(4)
    low_second, high_second = station(5)
    bits_first = ((high_first & 1) == 1, (high_first & 2) == 2)
    bits_second = ((high_second & 1) == 1, (high_second & 2) == 2)
    near_re = lookup(parts_re, low_first, bits_first)
    near_im = lookup(parts_im, low_first, bits_first)
    far_re = lookup(parts_re, low_second, bits_second)
    far_im = lookup(parts_im, low_second, bits_second)
    z_re = coh_re * far_re + coh_im * far_im
    z_im = coh_im * far_re - coh_re * far_im
    x_re = near_re * coh_re - near_im * coh_im
    x_im = near_re * coh_im + near_im * coh_re
    res_re = jnp.where(sublane < 2, misc, 0.0) - (near_re * z_re - near_im * z_im)
    res_im = jnp.where((sublane >= 2) & (sublane < 4), misc, 0.0) - (near_re * z_im + near_im * z_re)
    res_re = res_re + pltpu.roll(res_re, 4, 0)
    res_re = res_re + pltpu.roll(res_re, 2, 0)
    res_im = res_im + pltpu.roll(res_im, 4, 0)
    res_im = res_im + pltpu.roll(res_im, 2, 0)
    first = jnp.concatenate([res_re * z_re + res_im * z_im, res_im * z_re - res_re * z_im], 0)
    second = jnp.concatenate([res_re * x_re + res_im * x_im, res_re * x_im - res_im * x_re], 0)
    first_norm = z_re * z_re + z_im * z_im
    second_norm = x_re * x_re + x_im * x_im
    twice = lambda a: jnp.concatenate([a, a], 0).astype(bf16)
    return (
        (first.astype(bf16), twice(first_norm), low_first, high_first),
        (second.astype(bf16), twice(second_norm), low_second, high_second),
    )


def operands(term, station_rows, half_rows):
    pair, norm, low, high = term
    zero = jnp.zeros_like(pair)
    high = jnp.broadcast_to(high[:1].astype(f32), (16, LANES)).astype(bf16)
    rows = [jnp.where(high == float(h), pair, zero) for h in range(PARTS)]
    rows += [jnp.where(high == half_rows + float(h), norm, zero) for h in range(0, PARTS, 2)]
    low = jnp.broadcast_to(low[:1].astype(f32), (LANES, LANES)).astype(bf16)
    table = jnp.where(station_rows == low, jnp.ones_like(low), jnp.zeros_like(low))
    return jnp.concatenate(rows, 0), table


def accumulate(data_ref, gains_re, gains_im, sums_ref, acc_ref):
    sources, _, width = data_ref.shape
    chunk = min(CHUNK, width)
    per_source = width // chunk
    rounded_re = gains_re.astype(bf16).astype(f32)
    rounded_im = gains_im.astype(bf16).astype(f32)
    parts_re = [rounded_re[:, h * LANES : (h + 1) * LANES] for h in range(PARTS)]
    parts_im = [rounded_im[:, h * LANES : (h + 1) * LANES] for h in range(PARTS)]
    station_rows = lax.broadcasted_iota(i32, (LANES, LANES), 0).astype(f32).astype(bf16)
    half_rows = (lax.broadcasted_iota(i32, (16, LANES), 0) >> 3).astype(f32).astype(bf16)
    sublane = lax.broadcasted_iota(i32, (8, LANES), 0)
    acc_ref[...] = jnp.zeros_like(acc_ref)

    def step(index, carry):
        source = lax.div(index, per_source)
        offset = pl.multiple_of(lax.rem(index, per_source) * chunk, chunk)
        left, right = [], []
        for column in range(chunk // LANES):
            lanes = pl.ds(offset + column * LANES, LANES)
            coh_re = data_ref[source, 0:8, lanes].astype(f32)
            coh_im = data_ref[source, 8:16, lanes].astype(f32)
            misc = data_ref[source, 16:24, lanes].astype(f32)
            for term in column_terms(coh_re, coh_im, misc, parts_re, parts_im, sublane):
                rows, table = operands(term, station_rows, half_rows)
                left.append(rows)
                right.append(table)
        acc_ref[...] += lax.dot_general(
            jnp.concatenate(left, 1),
            jnp.concatenate(right, 1),
            (((1,), (1,)), ((), ())),
            preferred_element_type=f32,
        )
        return carry

    lax.fori_loop(0, sources * per_source, step, 0)
    acc = acc_ref[...]
    base = 16 * PARTS
    sums_ref[0] = jnp.concatenate([acc[16 * h : 16 * h + 8] for h in range(PARTS)], 1)
    sums_ref[1] = jnp.concatenate([acc[16 * h + 8 : 16 * h + 16] for h in range(PARTS)], 1)
    sums_ref[2] = jnp.concatenate([acc[base + 8 * h : base + 8 * h + 8] for h in range(PARTS)], 1)


def advance(gains, sums, target, penalty_weight):
    return gains + (sums[0:2] + penalty_weight * (target - gains)) / (
        2.0 * sums[2] + penalty_weight
    )


def sweep_kernel(data_ref, gains_ref, sums_ref, acc_ref):
    accumulate(data_ref, gains_ref[0], gains_ref[1], sums_ref, acc_ref)


def step_kernel(
    weight, data_ref, mine_ref, other_ref, gains_ref, target_ref, sums_ref, new_ref, acc_ref
):
    sums = mine_ref[...] + other_ref[...]
    gains = advance(gains_ref[...], sums, target_ref[...], weight)
    new_ref[...] = gains
    accumulate(data_ref, gains[0], gains[1], sums_ref, acc_ref)


def call(kernel, data, operands_in, out_shape, name):
    baselines = data.shape[0] * data.shape[2]
    whole = pl.BlockSpec(memory_space=pltpu.VMEM)
    return pl.pallas_call(
        kernel,
        out_shape=out_shape,
        in_specs=[whole] * (1 + len(operands_in)),
        out_specs=jax.tree.map(lambda _: whole, out_shape),
        scratch_shapes=[pltpu.VMEM((24 * PARTS, LANES), f32)],
        cost_estimate=pl.CostEstimate(
            flops=baselines * 24 * 2 * STATION_TOTAL * 2, bytes_accessed=data.size * 2, transcendentals=0
        ),
        name=name,
    )(data, *operands_in)


def shards(vis, coherency, gains_init, station_pairs):
    channels_dev = vis.shape[1]
    rows_dev = vis.shape[2]
    owned = gains_init.shape[3]
    pairs = lax.axis_size("pair")
    bands = lax.axis_size("freq")
    held = channels_dev // pairs
    assert held == 2 and STATION_TOTAL == 2 * owned * pairs
    stations = 2 * owned
    comps = 2 * SKY_DIRECTIONS * held
    weight = 2.0 * rows_dev * pairs * 2 / STATION_TOTAL
    swap = [(0, 1), (1, 0)]
    core = lax.axis_index("core")

    whole_basis = jnp.asarray(basis_rows(channels_dev * bands))
    local_basis = lax.dynamic_slice_in_dim(
        whole_basis, lax.axis_index("freq") * channels_dev, channels_dev, 1
    ).reshape(4, pairs, 1, 1, held, 1)

    def to_pairs(block):
        return lax.all_to_all(block, "pair", 0, 0, tiled=True)

    with jax.named_scope("pack"):
        gains_other = lax.ppermute(gains_init, "core", swap)
        gains_pair = jnp.where(
            core == 0,
            jnp.concatenate([gains_init, gains_other], 3),
            jnp.concatenate([gains_other, gains_init], 3),
        )
        gains_pair = gains_pair.reshape(2, SKY_DIRECTIONS, pairs, held, stations)
        gains_pair = gains_pair.transpose(2, 0, 1, 3, 4).reshape(pairs, comps * stations)
        upper = lax.reduce_precision(gains_pair, 8, 7)
        middle = lax.reduce_precision(gains_pair - upper, 8, 7)
        lower = gains_pair - upper - middle
        start = jnp.concatenate([upper, middle, lower], 1).astype(bf16)
        start = jnp.pad(start, ((0, 0), (0, 2 * rows_dev - start.shape[1]))).reshape(pairs, 2, rows_dev)
        coh = coherency.reshape(2, SKY_DIRECTIONS, pairs, held, rows_dev)
        coh = coh.transpose(2, 0, 1, 3, 4).reshape(pairs, comps, rows_dev)
        seen = vis.astype(bf16).reshape(2, pairs, held, rows_dev)
        seen = seen.transpose(1, 0, 2, 3).reshape(pairs, 2 * held, rows_dev)
        codes = (station_pairs - STATION_TOTAL // 2).astype(bf16)
        codes = jnp.broadcast_to(codes, (pairs, 2, rows_dev))
        packed = jnp.concatenate([coh, seen, codes, start], 1)
    with jax.named_scope("regroup"):
        data = to_pairs(packed)
    with jax.named_scope("unpack"):
        start = data[:, 22:24].reshape(pairs, 2 * rows_dev)[:, : 3 * comps * stations]
        start = start.astype(f32).reshape(pairs, 3, comps, stations)
        start = start[:, 0] + start[:, 1] + start[:, 2]

    def by_channel(block):
        return block.transpose(1, 0, 2).reshape(2, comps // 2, STATION_TOTAL)

    def by_station(values):
        block = values.reshape(comps, pairs, stations).transpose(1, 0, 2)
        block = to_pairs(block)
        return block.reshape(pairs, 2, SKY_DIRECTIONS, held, stations)

    sums_shape = jax.ShapeDtypeStruct((3, comps // 2, STATION_TOTAL), f32)
    gains_shape = jax.ShapeDtypeStruct((2, comps // 2, STATION_TOTAL), f32)

    gains = by_channel(start)
    target = gains
    dual = jnp.zeros_like(gains)
    owner_dual = jnp.zeros((pairs, 2, SKY_DIRECTIONS, held, stations), f32)
    partial = call(sweep_kernel, data, (gains,), sums_shape, "sweep")
    for round_index in range(ROUNDS):
        for step_index in range(ITERS):
            other = lax.ppermute(partial, "core", swap)
            if step_index < ITERS - 1:
                partial, gains = call(
                    functools.partial(step_kernel, weight),
                    data,
                    (partial, other, gains, target),
                    (sums_shape, gains_shape),
                    "step",
                )
            else:
                gains = advance(gains, partial + other, target, weight)
        last = round_index == ROUNDS - 1
        if not last:
            partial = call(sweep_kernel, data, (gains,), sums_shape, "sweep")
        with jax.named_scope("fit"):
            owner_gains = by_station(gains)
            blend = owner_gains + owner_dual
            part = jnp.sum(local_basis * blend[None], axis=(1, 4)).reshape(1, 8, LANES)
            part = jnp.broadcast_to(part, (bands, 8, LANES))
            part = lax.all_to_all(part, "freq", 0, 0, tiled=True)
            coefficients = jnp.sum(part, 0).reshape(4, 1, 2, SKY_DIRECTIONS, 1, stations)
            owner_consensus = jnp.sum(local_basis * coefficients, axis=0)
        if not last:
            with jax.named_scope("spread"):
                owner_dual = owner_dual + owner_gains - owner_consensus
                consensus = by_channel(to_pairs(owner_consensus.reshape(pairs, comps, stations)))
                dual = dual + gains - consensus
                target = consensus - dual

    def placed(block):
        block = block.transpose(1, 2, 0, 3, 4).reshape(2, SKY_DIRECTIONS, channels_dev, stations)
        return lax.dynamic_slice_in_dim(block, core * owned, owned, 3)

    return (placed(owner_gains), placed(owner_consensus))


def solution(mesh):
    split = Mesh(
        mesh.devices.reshape(mesh.shape["freq"], mesh.shape["bl"] // 2, 2), ("freq", "pair", "core")
    )
    bl = ("pair", "core")
    placed = (
        P(None, "freq", bl),
        P(None, None, "freq", bl),
        P(None, None, "freq", bl),
        P(None, bl),
    )
    return jax.shard_map(
        shards,
        mesh=split,
        in_specs=placed,
        out_specs=(P(None, None, "freq", bl), P(None, None, "freq", bl)),
        check_vma=False,
    )
```

```python
import functools

import jax
import jax.numpy as jnp
import numpy as np
from jax import lax
from jax.experimental import pallas as pl
from jax.experimental.pallas import tpu as pltpu
from jax.sharding import Mesh, PartitionSpec as P

STATION_TOTAL = 512
SKY_DIRECTIONS = 4
ITERS = 2
ROUNDS = 2
LANES = 128
PARTS = STATION_TOTAL // LANES
UNROLL = 2
VMEM_LIMIT = 24 * 1024 * 1024
f32, bf16, i32 = jnp.float32, jnp.bfloat16, jnp.int32


def basis_rows(channels):
    position = (2.0 * np.arange(channels) + 1.0) / channels - 1.0
    rows = []
    for vector in [np.ones_like(position), position, position**2, position**3]:
        for other in rows:
            vector = vector - np.sum(other * vector) * other
        rows.append(vector / np.sqrt(np.sum(vector * vector)))
    return np.stack(rows).astype(np.float32)


def lanes_of(rows):
    return {"re": 0, "im": rows, "misc": 2 * rows, "low": 3 * rows, "start": 3 * rows + rows // 2}


def pick_channel_pair(by_direction, pair):
    return jnp.concatenate([block[2 * pair : 2 * pair + 2] for block in by_direction], 0)


def pack_kernel(core_ref, coh_ref, vis_ref, pairs_ref, mine_ref, other_ref, out_ref):
    rows = vis_ref.shape[2]
    count = out_ref.shape[0]
    at = lanes_of(rows)
    half = rows // 2

    def columns(index, carry):
        early = pl.multiple_of(index * LANES, LANES)
        late = pl.multiple_of(half + index * LANES, LANES)
        lower = []
        for offset in (early, late):
            lanes = pl.ds(offset, LANES)
            for part in range(2):
                blocks = [coh_ref[part, d, :, lanes].astype(f32) for d in range(SKY_DIRECTIONS)]
                place = pl.multiple_of(offset + part * rows, LANES)
                for p in range(count):
                    out_ref[p, :, pl.ds(place, LANES)] = pick_channel_pair(blocks, p).astype(bf16)
            upper = []
            for part in range(2):
                seen = vis_ref[part, :, lanes]
                rounded = seen.astype(bf16).astype(f32)
                upper.append(rounded)
                lower.append(seen - rounded)
            codes = (pairs_ref[:, lanes] - STATION_TOTAL // 2).astype(f32)
            tail = jnp.concatenate([codes, jnp.zeros((2, LANES), f32)], 0)
            place = pl.multiple_of(offset + at["misc"], LANES)
            for p in range(count):
                block = jnp.concatenate([upper[0][2 * p : 2 * p + 2], upper[1][2 * p : 2 * p + 2], tail], 0)
                out_ref[p, :, pl.ds(place, LANES)] = block.astype(bf16)
        place = pl.multiple_of(early + at["low"], LANES)
        for p in range(count):
            out_ref[p, :, pl.ds(place, LANES)] = pick_channel_pair(lower, p).astype(bf16)
        return carry

    lax.fori_loop(0, half // LANES, columns, 0)
    is_first = core_ref[0] == 0
    for part in range(2):
        mine = jnp.concatenate([mine_ref[part, d] for d in range(SKY_DIRECTIONS)], 1)
        other = jnp.concatenate([other_ref[part, d] for d in range(SKY_DIRECTIONS)], 1)
        start = jnp.concatenate([jnp.where(is_first, mine, other), jnp.where(is_first, other, mine)], 0)
        upper = start.astype(bf16).astype(f32)
        middle = (start - upper).astype(bf16).astype(f32)
        lower = start - upper - middle
        square = jnp.concatenate([upper, middle, lower, jnp.zeros_like(start)], 0).T
        blocks = [square[d * 2 * count : (d + 1) * 2 * count] for d in range(SKY_DIRECTIONS)]
        place = at["start"] + part * LANES
        for p in range(count):
            out_ref[p, :, place : place + LANES] = pick_channel_pair(blocks, p).astype(bf16)


def stations_in_lanes(pieces):
    lane = lax.broadcasted_iota(i32, (8, LANES), 1)
    tiles = []
    for q in range(0, len(pieces), 4):
        tile = pieces[q]
        for k in range(1, 4):
            moved = pltpu.roll(pieces[q + k], 32 * k, 1)
            tile = jnp.where(lane >= 32 * k, moved, tile)
        tiles.append(tile)
    return jnp.concatenate(tiles, 1)


def starting_gains(data_ref):
    at = lanes_of((data_ref.shape[2] - 2 * LANES) * 2 // 7)["start"]
    parts = []
    for part in range(2):
        pieces = []
        for p in range(data_ref.shape[0]):
            piece = data_ref[p, :, at + part * LANES : at + (part + 1) * LANES].astype(f32)
            piece = piece + pltpu.roll(piece, LANES - 32, 1) + pltpu.roll(piece, LANES - 64, 1)
            pieces.append(piece)
        parts.append(stations_in_lanes(pieces))
    return parts


def lookup(parts, low, bits):
    picked = [jnp.take_along_axis(p, low, axis=1, mode="promise_in_bounds") for p in parts]
    return jnp.where(
        bits[1], jnp.where(bits[0], picked[3], picked[2]), jnp.where(bits[0], picked[1], picked[0])
    )


def column_terms(coh_re, coh_im, misc, low, low_row, parts_re, parts_im, sublane):
    def station(row):
        index = jnp.broadcast_to((misc[row : row + 1] + 256.0).astype(i32), (8, LANES))
        return index & (LANES - 1), index >> 7

    low_first, high_first = station(4)
    low_second, high_second = station(5)
    bits_first = ((high_first & 1) == 1, (high_first & 2) == 2)
    bits_second = ((high_second & 1) == 1, (high_second & 2) == 2)
    near_re = lookup(parts_re, low_first, bits_first)
    near_im = lookup(parts_im, low_first, bits_first)
    far_re = lookup(parts_re, low_second, bits_second)
    far_im = lookup(parts_im, low_second, bits_second)
    z_re = coh_re * far_re + coh_im * far_im
    z_im = coh_im * far_re - coh_re * far_im
    x_re = near_re * coh_re - near_im * coh_im
    x_im = near_re * coh_im + near_im * coh_re
    inside = lambda row: (sublane >= row) & (sublane < row + 2)
    vis_re = jnp.where(inside(0), misc, jnp.where(inside(low_row), low, 0.0))
    vis_im = jnp.where(inside(2), misc, jnp.where(inside(low_row + 2), low, 0.0))
    if low_row == 0:
        vis_re = jnp.where(inside(0), misc + low, 0.0)
        vis_im = jnp.where(inside(2), misc + low, 0.0)
    res_re = vis_re - (near_re * z_re - near_im * z_im)
    res_im = vis_im - (near_re * z_im + near_im * z_re)
    res_re = res_re + pltpu.roll(res_re, 4, 0)
    res_re = res_re + pltpu.roll(res_re, 2, 0)
    res_im = res_im + pltpu.roll(res_im, 4, 0)
    res_im = res_im + pltpu.roll(res_im, 2, 0)
    first = jnp.concatenate([res_re * z_re + res_im * z_im, res_im * z_re - res_re * z_im], 0)
    second = jnp.concatenate([res_re * x_re + res_im * x_im, res_re * x_im - res_im * x_re], 0)
    first_norm = z_re * z_re + z_im * z_im
    second_norm = x_re * x_re + x_im * x_im
    twice = lambda a: jnp.concatenate([a, a], 0).astype(bf16)
    return (
        (first.astype(bf16), twice(first_norm), low_first, high_first),
        (second.astype(bf16), twice(second_norm), low_second, high_second),
    )


def operands(term, station_rows, half_rows):
    pair, norm, low, high = term
    zero = jnp.zeros_like(pair)
    high = jnp.broadcast_to(high[:1].astype(f32), (16, LANES)).astype(bf16)
    rows = [jnp.where(high == float(h), pair, zero) for h in range(PARTS)]
    rows += [jnp.where(high == half_rows + float(h), norm, zero) for h in range(0, PARTS, 2)]
    low = jnp.broadcast_to(low[:1].astype(f32), (LANES, LANES)).astype(bf16)
    table = jnp.where(station_rows == low, jnp.ones_like(low), jnp.zeros_like(low))
    return jnp.concatenate(rows, 0), table


def accumulate(data_ref, first, count, gains_re, gains_im, sums_ref, acc_ref, before=None):
    rows = (data_ref.shape[2] - 2 * LANES) * 2 // 7
    at = lanes_of(rows)
    half = rows // 2
    rounded_re = gains_re.astype(bf16).astype(f32)
    rounded_im = gains_im.astype(bf16).astype(f32)
    parts_re = [rounded_re[:, h * LANES : (h + 1) * LANES] for h in range(PARTS)]
    parts_im = [rounded_im[:, h * LANES : (h + 1) * LANES] for h in range(PARTS)]
    station_rows = lax.broadcasted_iota(i32, (LANES, LANES), 0).astype(f32).astype(bf16)
    half_rows = (lax.broadcasted_iota(i32, (16, LANES), 0) >> 3).astype(f32).astype(bf16)
    sublane = lax.broadcasted_iota(i32, (8, LANES), 0)
    acc_ref[...] = jnp.zeros_like(acc_ref)

    def step(source, carry):
        left, right = [], []
        for offset in range(0, rows, LANES):
            load = lambda start: data_ref[source, :, start : start + LANES].astype(f32)
            low = load(at["low"] + offset % half)
            terms = column_terms(
                load(at["re"] + offset),
                load(at["im"] + offset),
                load(at["misc"] + offset),
                low,
                4 * (offset // half),
                parts_re,
                parts_im,
                sublane,
            )
            (rows_first, table_first), (rows_second, table_second) = [
                operands(term, station_rows, half_rows) for term in terms
            ]
            left.append(jnp.concatenate([rows_first, rows_second], 0))
            right.append(jnp.concatenate([table_first, table_second], 0))
        acc_ref[...] += lax.dot_general(
            jnp.concatenate(left, 1),
            jnp.concatenate(right, 1),
            (((1,), (1,)), ((), ())),
            preferred_element_type=f32,
        )
        return carry

    lax.fori_loop(first, first + count, step, 0, unroll=UNROLL)
    tall = 24 * PARTS
    acc = acc_ref[0:tall, 0:LANES] + acc_ref[tall : 2 * tall, LANES : 2 * LANES]
    base = 16 * PARTS
    sums = [
        jnp.concatenate([acc[16 * h : 16 * h + 8] for h in range(PARTS)], 1),
        jnp.concatenate([acc[16 * h + 8 : 16 * h + 16] for h in range(PARTS)], 1),
        jnp.concatenate([acc[base + 8 * h : base + 8 * h + 8] for h in range(PARTS)], 1),
    ]
    for k in range(3):
        sums_ref[k] = sums[k] if before is None else before[k] + sums[k]


def advance(gains, sums, target, penalty_weight):
    return gains + (sums[0:2] + penalty_weight * (target - gains)) / (
        2.0 * sums[2] + penalty_weight
    )


def first_kernel(data_ref, sums_ref, gains_ref, acc_ref):
    gains = starting_gains(data_ref)
    gains_ref[0], gains_ref[1] = gains
    accumulate(data_ref, 0, data_ref.shape[0], *gains, sums_ref, acc_ref)


def early_kernel(data_ref, gains_ref, sums_ref, acc_ref):
    accumulate(data_ref, 0, data_ref.shape[0] // 2, gains_ref[0], gains_ref[1], sums_ref, acc_ref)


def late_kernel(data_ref, gains_ref, before_ref, sums_ref, acc_ref):
    half = data_ref.shape[0] // 2
    accumulate(data_ref, half, half, gains_ref[0], gains_ref[1], sums_ref, acc_ref, before_ref)


def step_kernel(weight, data_ref, mine_ref, other_ref, gains_ref, sums_ref, new_ref, acc_ref):
    gains = gains_ref[...]
    gains = advance(gains, mine_ref[...] + other_ref[...], gains, weight)
    new_ref[...] = gains
    accumulate(data_ref, 0, data_ref.shape[0], gains[0], gains[1], sums_ref, acc_ref)


def retarget_kernel(
    weight, data_ref, mine_ref, other_ref, gains_ref, fit_ref, sums_ref, new_ref, target_ref, acc_ref
):
    consensus = by_channel(fit_ref)
    gains = gains_ref[...]
    target = consensus - (gains - consensus)
    target_ref[...] = target
    gains = advance(gains, mine_ref[...] + other_ref[...], target, weight)
    new_ref[...] = gains
    accumulate(data_ref, 0, data_ref.shape[0], gains[0], gains[1], sums_ref, acc_ref)


def by_channel(block_ref):
    pieces = [block_ref[p] for p in range(block_ref.shape[0])]
    turned = [pltpu.roll(piece, LANES - 32, 1) for piece in pieces]
    return jnp.stack([stations_in_lanes(pieces), stations_in_lanes(turned)])


def finish_kernel(weight, mine_ref, other_ref, gains_ref, target_ref, new_ref, block_ref):
    gains = advance(gains_ref[...], mine_ref[...] + other_ref[...], target_ref[...], weight)
    new_ref[...] = gains
    lane = lax.broadcasted_iota(i32, (8, LANES), 1)
    for p in range(block_ref.shape[0]):
        tile = slice(p // 4 * LANES, (p // 4 + 1) * LANES)
        shift = 32 * (p % 4)
        real = pltpu.roll(gains[0][:, tile], (LANES - shift) % LANES, 1)
        imag = pltpu.roll(gains[1][:, tile], (LANES + 32 - shift) % LANES, 1)
        block_ref[p] = jnp.where(lane < 32, real, imag)


def is_even(shape):
    return (lax.broadcasted_iota(i32, shape, 0) & 1) == 0


def basis_column(basis_ref, row, source):
    even = is_even((8, LANES))
    return jnp.where(even, basis_ref[row, 2 * source], basis_ref[row, 2 * source + 1])


def fit_kernel(basis_ref, *refs):
    *block_refs, out_ref = refs
    even = is_even((8, LANES))
    blocks = []
    for p in range(block_refs[0].shape[0]):
        blend = block_refs[0][p]
        if len(block_refs) > 1:
            blend = blend + block_refs[1][p]
        blocks.append(blend)
    totals = []
    for row in range(4):
        total = sum(basis_column(basis_ref, row, p) * block for p, block in enumerate(blocks))
        totals.append(total + jnp.where(even, pltpu.roll(total, 7, 0), pltpu.roll(total, 1, 0)))
    lane = lax.broadcasted_iota(i32, (8, LANES), 1)
    early = jnp.where(even, totals[0], totals[1])
    late = jnp.where(even, totals[2], totals[3])
    packed = jnp.where(lane < LANES // 2, early, pltpu.roll(late, LANES // 2, 1))
    for f in range(out_ref.shape[0]):
        out_ref[f] = packed


def consensus_blocks(basis_ref, parts_ref, count):
    even = is_even((8, LANES))
    total = parts_ref[0]
    for f in range(1, parts_ref.shape[0]):
        total = total + parts_ref[f]
    rows = []
    for half in (total, pltpu.roll(total, LANES // 2, 1)):
        rows.append(jnp.where(even, half, pltpu.roll(half, 1, 0)))
        rows.append(jnp.where(even, pltpu.roll(half, 7, 0), half))
    return [
        sum(basis_column(basis_ref, row, p) * rows[row] for row in range(4)) for p in range(count)
    ]


def spread_kernel(basis_ref, parts_ref, gains_ref, out_ref, dual_ref):
    for p, block in enumerate(consensus_blocks(basis_ref, parts_ref, out_ref.shape[0])):
        out_ref[p] = block
        dual_ref[p] = gains_ref[p] - block


def write_owned(blocks, is_first, out_ref):
    owned = out_ref.shape[2]
    channels = 2 * len(blocks)
    rows = [block[2 * d : 2 * d + 2] for d in range(SKY_DIRECTIONS) for block in blocks]
    turned = jnp.concatenate(rows, 0).T
    for part in range(2):
        both = turned[part * 2 * owned : (part + 1) * 2 * owned]
        mine = jnp.where(is_first, both[:owned], both[owned:])
        for d in range(SKY_DIRECTIONS):
            out_ref[part, d] = mine[:, d * channels : (d + 1) * channels]


def place_kernel(core_ref, blocks_ref, out_ref):
    write_owned([blocks_ref[p] for p in range(blocks_ref.shape[0])], core_ref[0] == 0, out_ref)


def final_kernel(basis_ref, core_ref, parts_ref, out_ref):
    count = out_ref.shape[3] // 2
    write_owned(consensus_blocks(basis_ref, parts_ref, count), core_ref[0] == 0, out_ref)


def call(name, kernel, out_shape, *inputs, scalars=0, flops=0, scratch=()):
    whole = pl.BlockSpec(memory_space=pltpu.VMEM)
    specs = [pl.BlockSpec(memory_space=pltpu.SMEM)] * scalars + [whole] * (len(inputs) - scalars)
    return pl.pallas_call(
        kernel,
        out_shape=out_shape,
        in_specs=specs,
        out_specs=jax.tree.map(lambda _: whole, out_shape),
        scratch_shapes=list(scratch),
        compiler_params=pltpu.CompilerParams(vmem_limit_bytes=VMEM_LIMIT),
        cost_estimate=pl.CostEstimate(
            flops=flops, bytes_accessed=sum(x.size * x.dtype.itemsize for x in inputs), transcendentals=0
        ),
        name=name,
    )(*inputs)


def shards(vis, coherency, gains_init, station_pairs):
    channels_dev = vis.shape[1]
    rows_dev = vis.shape[2]
    owned = gains_init.shape[3]
    pairs = lax.axis_size("pair")
    bands = lax.axis_size("freq")
    assert channels_dev == 2 * pairs and owned == 16 and STATION_TOTAL == 2 * owned * pairs
    assert ROUNDS == 2 and ITERS == 2
    weight = 2.0 * rows_dev * pairs * 2 / STATION_TOTAL
    swap = [(0, 1), (1, 0)]
    core = lax.axis_index("core").astype(i32).reshape(1)
    basis = lax.dynamic_slice_in_dim(
        jnp.asarray(basis_rows(channels_dev * bands)),
        lax.axis_index("freq") * channels_dev,
        channels_dev,
        1,
    )
    shape = jax.ShapeDtypeStruct
    gains_shape = shape((2, 8, STATION_TOTAL), f32)
    sums_shape = shape((3, 8, STATION_TOTAL), f32)
    block_shape = shape((pairs, 8, LANES), f32)
    parts_shape = shape((bands, 8, LANES), f32)
    out_shape = shape((2, SKY_DIRECTIONS, owned, channels_dev), f32)
    width = 7 * rows_dev // 2 + 2 * LANES
    flops = 2 * rows_dev * pairs * 192 * 256
    scratch = [pltpu.VMEM((48 * PARTS, 2 * LANES), f32)]
    sweep = functools.partial(call, flops=flops, scratch=scratch)
    half_sweep = functools.partial(call, flops=flops // 2, scratch=scratch)

    def exchange(partial):
        return lax.ppermute(partial, "core", swap)

    def to_pairs(block):
        return lax.all_to_all(block, "pair", 0, 0, tiled=True)

    def over_bands(block):
        return lax.all_to_all(block, "freq", 0, 0, tiled=True)

    start = gains_init.transpose(0, 1, 3, 2)
    packed = call(
        "pack",
        pack_kernel,
        shape((pairs, 8, width), bf16),
        core,
        coherency,
        vis,
        station_pairs,
        start,
        exchange(start),
        scalars=1,
    )
    data = to_pairs(packed)

    sums, gains = sweep("first", first_kernel, (sums_shape, gains_shape), data)
    target = gains
    sums, gains = sweep(
        "step",
        functools.partial(step_kernel, weight),
        (sums_shape, gains_shape),
        data,
        sums,
        exchange(sums),
        gains,
    )
    finish = functools.partial(finish_kernel, weight)
    gains, block = call("finish", finish, (gains_shape, block_shape), sums, exchange(sums), gains, target)
    owner_gains = to_pairs(block)
    sums = half_sweep("early", early_kernel, sums_shape, data, gains)
    parts = over_bands(call("fit", fit_kernel, parts_shape, basis, owner_gains, scalars=1))
    sums = half_sweep("late", late_kernel, sums_shape, data, gains, sums)
    block, owner_dual = call(
        "spread", spread_kernel, (block_shape, block_shape), basis, parts, owner_gains, scalars=1
    )
    fit = to_pairs(block)

    sums, gains, target = sweep(
        "retarget",
        functools.partial(retarget_kernel, weight),
        (sums_shape, gains_shape, gains_shape),
        data,
        sums,
        exchange(sums),
        gains,
        fit,
    )
    gains, block = call("finish", finish, (gains_shape, block_shape), sums, exchange(sums), gains, target)
    owner_gains = to_pairs(block)
    parts = over_bands(call("fit", fit_kernel, parts_shape, basis, owner_gains, owner_dual, scalars=1))
    final_gains = call("place", place_kernel, out_shape, core, owner_gains, scalars=1)
    final_consensus = call("final", final_kernel, out_shape, basis, core, parts, scalars=2)
    return (final_gains.transpose(0, 1, 3, 2), final_consensus.transpose(0, 1, 3, 2))


def solution(mesh):
    split = Mesh(
        mesh.devices.reshape(mesh.shape["freq"], mesh.shape["bl"] // 2, 2), ("freq", "pair", "core")
    )
    bl = ("pair", "core")
    placed = (
        P(None, "freq", bl),
        P(None, None, "freq", bl),
        P(None, None, "freq", bl),
        P(None, bl),
    )
    return jax.shard_map(
        shards,
        mesh=split,
        in_specs=placed,
        out_specs=(P(None, None, "freq", bl), P(None, None, "freq", bl)),
        check_vma=False,
    )
```

```python
import functools

import jax
import jax.numpy as jnp
import numpy as np
from jax import lax
from jax.experimental import pallas as pl
from jax.experimental.pallas import tpu as pltpu
from jax.sharding import Mesh, PartitionSpec as P

STATION_TOTAL = 512
SKY_DIRECTIONS = 4
ITERS = 2
ROUNDS = 2
LANES = 128
PARTS = STATION_TOTAL // LANES
UNROLL = 2
COPIES = 4
PACK_VMEM_LIMIT = 58 * 1024 * 1024
VMEM_LIMIT = 24 * 1024 * 1024
f32, bf16, i32 = jnp.float32, jnp.bfloat16, jnp.int32


def basis_rows(channels):
    position = (2.0 * np.arange(channels) + 1.0) / channels - 1.0
    rows = []
    for vector in [np.ones_like(position), position, position**2, position**3]:
        for other in rows:
            vector = vector - np.sum(other * vector) * other
        rows.append(vector / np.sqrt(np.sum(vector * vector)))
    return np.stack(rows).astype(np.float32)


def lanes_of(rows):
    return {"re": 0, "im": rows, "misc": 2 * rows, "low": 3 * rows, "start": 3 * rows + rows // 2}


def pick_channel_pair(by_direction, pair):
    return jnp.concatenate([block[2 * pair : 2 * pair + 2] for block in by_direction], 0)


def pack_kernel(
    core_ref, coh_hbm, vis_hbm, pairs_ref, mine_ref, other_ref, out_ref, coh_ref, vis_ref, coh_sem, vis_sem
):
    rows = vis_ref.shape[2]
    count = out_ref.shape[0]
    at = lanes_of(rows)
    half = rows // 2
    piece = half // COPIES
    copies = []
    for index in range(COPIES):
        group = []
        for side in range(2):
            lanes = pl.ds(side * half + index * piece, piece)
            slot = 2 * index + side
            group.append(
                pltpu.make_async_copy(
                    coh_hbm.at[:, :, :, lanes], coh_ref.at[:, :, :, lanes], coh_sem.at[slot]
                )
            )
            group.append(
                pltpu.make_async_copy(vis_hbm.at[:, :, lanes], vis_ref.at[:, :, lanes], vis_sem.at[slot])
            )
        for copy in group:
            copy.start()
        copies.append(group)

    def columns(index, carry):
        early = pl.multiple_of(index * LANES, LANES)
        late = pl.multiple_of(half + index * LANES, LANES)
        lower = []
        for offset in (early, late):
            lanes = pl.ds(offset, LANES)
            for part in range(2):
                blocks = [coh_ref[part, d, :, lanes].astype(f32) for d in range(SKY_DIRECTIONS)]
                place = pl.multiple_of(offset + part * rows, LANES)
                for p in range(count):
                    out_ref[p, :, pl.ds(place, LANES)] = pick_channel_pair(blocks, p).astype(bf16)
            upper = []
            for part in range(2):
                seen = vis_ref[part, :, lanes]
                rounded = seen.astype(bf16).astype(f32)
                upper.append(rounded)
                lower.append(seen - rounded)
            codes = (pairs_ref[:, lanes] - STATION_TOTAL // 2).astype(f32)
            tail = jnp.concatenate([codes, jnp.zeros((2, LANES), f32)], 0)
            place = pl.multiple_of(offset + at["misc"], LANES)
            for p in range(count):
                block = jnp.concatenate([upper[0][2 * p : 2 * p + 2], upper[1][2 * p : 2 * p + 2], tail], 0)
                out_ref[p, :, pl.ds(place, LANES)] = block.astype(bf16)
        place = pl.multiple_of(early + at["low"], LANES)
        for p in range(count):
            out_ref[p, :, pl.ds(place, LANES)] = pick_channel_pair(lower, p).astype(bf16)
        return carry

    is_first = core_ref[0] == 0
    for part in range(2):
        mine = jnp.concatenate([mine_ref[part, d] for d in range(SKY_DIRECTIONS)], 1)
        other = jnp.concatenate([other_ref[part, d] for d in range(SKY_DIRECTIONS)], 1)
        start = jnp.concatenate([jnp.where(is_first, mine, other), jnp.where(is_first, other, mine)], 0)
        upper = start.astype(bf16).astype(f32)
        middle = (start - upper).astype(bf16).astype(f32)
        lower = start - upper - middle
        square = jnp.concatenate([upper, middle, lower, jnp.zeros_like(start)], 0).T
        blocks = [square[d * 2 * count : (d + 1) * 2 * count] for d in range(SKY_DIRECTIONS)]
        place = at["start"] + part * LANES
        for p in range(count):
            out_ref[p, :, place : place + LANES] = pick_channel_pair(blocks, p).astype(bf16)
    step = piece // LANES
    for index, group in enumerate(copies):
        for copy in group:
            copy.wait()
        lax.fori_loop(index * step, (index + 1) * step, columns, 0)


def stations_in_lanes(pieces):
    lane = lax.broadcasted_iota(i32, (8, LANES), 1)
    tiles = []
    for q in range(0, len(pieces), 4):
        tile = pieces[q]
        for k in range(1, 4):
            moved = pltpu.roll(pieces[q + k], 32 * k, 1)
            tile = jnp.where(lane >= 32 * k, moved, tile)
        tiles.append(tile)
    return jnp.concatenate(tiles, 1)


def starting_gains(data_ref):
    at = lanes_of((data_ref.shape[2] - 2 * LANES) * 2 // 7)["start"]
    parts = []
    for part in range(2):
        pieces = []
        for p in range(data_ref.shape[0]):
            piece = data_ref[p, :, at + part * LANES : at + (part + 1) * LANES].astype(f32)
            piece = piece + pltpu.roll(piece, LANES - 32, 1) + pltpu.roll(piece, LANES - 64, 1)
            pieces.append(piece)
        parts.append(stations_in_lanes(pieces))
    return parts


def lookup(parts, low, bits):
    picked = [jnp.take_along_axis(p, low, axis=1, mode="promise_in_bounds") for p in parts]
    return jnp.where(
        bits[1], jnp.where(bits[0], picked[3], picked[2]), jnp.where(bits[0], picked[1], picked[0])
    )


def column_terms(coh_re, coh_im, misc, low, low_row, parts_re, parts_im, sublane):
    def station(row):
        index = jnp.broadcast_to((misc[row : row + 1] + 256.0).astype(i32), (8, LANES))
        return index & (LANES - 1), index >> 7

    low_first, high_first = station(4)
    low_second, high_second = station(5)
    bits_first = ((high_first & 1) == 1, (high_first & 2) == 2)
    bits_second = ((high_second & 1) == 1, (high_second & 2) == 2)
    near_re = lookup(parts_re, low_first, bits_first)
    near_im = lookup(parts_im, low_first, bits_first)
    far_re = lookup(parts_re, low_second, bits_second)
    far_im = lookup(parts_im, low_second, bits_second)
    z_re = coh_re * far_re + coh_im * far_im
    z_im = coh_im * far_re - coh_re * far_im
    x_re = near_re * coh_re - near_im * coh_im
    x_im = near_re * coh_im + near_im * coh_re
    inside = lambda row: (sublane >= row) & (sublane < row + 2)
    vis_re = jnp.where(inside(0), misc, jnp.where(inside(low_row), low, 0.0))
    vis_im = jnp.where(inside(2), misc, jnp.where(inside(low_row + 2), low, 0.0))
    if low_row == 0:
        vis_re = jnp.where(inside(0), misc + low, 0.0)
        vis_im = jnp.where(inside(2), misc + low, 0.0)
    res_re = vis_re - (near_re * z_re - near_im * z_im)
    res_im = vis_im - (near_re * z_im + near_im * z_re)
    res_re = res_re + pltpu.roll(res_re, 4, 0)
    res_re = res_re + pltpu.roll(res_re, 2, 0)
    res_im = res_im + pltpu.roll(res_im, 4, 0)
    res_im = res_im + pltpu.roll(res_im, 2, 0)
    first = jnp.concatenate([res_re * z_re + res_im * z_im, res_im * z_re - res_re * z_im], 0)
    second = jnp.concatenate([res_re * x_re + res_im * x_im, res_re * x_im - res_im * x_re], 0)
    first_norm = z_re * z_re + z_im * z_im
    second_norm = x_re * x_re + x_im * x_im
    twice = lambda a: jnp.concatenate([a, a], 0).astype(bf16)
    return (
        (first.astype(bf16), twice(first_norm), low_first, high_first),
        (second.astype(bf16), twice(second_norm), low_second, high_second),
    )


def operands(term, station_rows, half_rows):
    pair, norm, low, high = term
    zero = jnp.zeros_like(pair)
    high = jnp.broadcast_to(high[:1].astype(f32), (16, LANES)).astype(bf16)
    rows = [jnp.where(high == float(h), pair, zero) for h in range(PARTS)]
    rows += [jnp.where(high == half_rows + float(h), norm, zero) for h in range(0, PARTS, 2)]
    low = jnp.broadcast_to(low[:1].astype(f32), (LANES, LANES)).astype(bf16)
    table = jnp.where(station_rows == low, jnp.ones_like(low), jnp.zeros_like(low))
    return jnp.concatenate(rows, 0), table


def accumulate(data_ref, first, count, gains_re, gains_im, sums_ref, acc_ref, before=None):
    rows = (data_ref.shape[2] - 2 * LANES) * 2 // 7
    at = lanes_of(rows)
    half = rows // 2
    rounded_re = gains_re.astype(bf16).astype(f32)
    rounded_im = gains_im.astype(bf16).astype(f32)
    parts_re = [rounded_re[:, h * LANES : (h + 1) * LANES] for h in range(PARTS)]
    parts_im = [rounded_im[:, h * LANES : (h + 1) * LANES] for h in range(PARTS)]
    station_rows = lax.broadcasted_iota(i32, (LANES, LANES), 0).astype(f32).astype(bf16)
    half_rows = (lax.broadcasted_iota(i32, (16, LANES), 0) >> 3).astype(f32).astype(bf16)
    sublane = lax.broadcasted_iota(i32, (8, LANES), 0)
    acc_ref[...] = jnp.zeros_like(acc_ref)

    def step(source, carry):
        left, right = [], []
        for offset in range(0, rows, LANES):
            load = lambda start: data_ref[source, :, start : start + LANES].astype(f32)
            low = load(at["low"] + offset % half)
            terms = column_terms(
                load(at["re"] + offset),
                load(at["im"] + offset),
                load(at["misc"] + offset),
                low,
                4 * (offset // half),
                parts_re,
                parts_im,
                sublane,
            )
            (rows_first, table_first), (rows_second, table_second) = [
                operands(term, station_rows, half_rows) for term in terms
            ]
            left.append(jnp.concatenate([rows_first, rows_second], 0))
            right.append(jnp.concatenate([table_first, table_second], 0))
        acc_ref[...] += lax.dot_general(
            jnp.concatenate(left, 1),
            jnp.concatenate(right, 1),
            (((1,), (1,)), ((), ())),
            preferred_element_type=f32,
        )
        return carry

    lax.fori_loop(first, first + count, step, 0, unroll=UNROLL)
    tall = 24 * PARTS
    acc = acc_ref[0:tall, 0:LANES] + acc_ref[tall : 2 * tall, LANES : 2 * LANES]
    base = 16 * PARTS
    sums = [
        jnp.concatenate([acc[16 * h : 16 * h + 8] for h in range(PARTS)], 1),
        jnp.concatenate([acc[16 * h + 8 : 16 * h + 16] for h in range(PARTS)], 1),
        jnp.concatenate([acc[base + 8 * h : base + 8 * h + 8] for h in range(PARTS)], 1),
    ]
    for k in range(3):
        sums_ref[k] = sums[k] if before is None else before[k] + sums[k]


def advance(gains, sums, target, penalty_weight):
    return gains + (sums[0:2] + penalty_weight * (target - gains)) / (
        2.0 * sums[2] + penalty_weight
    )


def first_kernel(data_ref, sums_ref, gains_ref, acc_ref):
    gains = starting_gains(data_ref)
    gains_ref[0], gains_ref[1] = gains
    accumulate(data_ref, 0, data_ref.shape[0], *gains, sums_ref, acc_ref)


def early_kernel(data_ref, gains_ref, sums_ref, acc_ref):
    accumulate(data_ref, 0, data_ref.shape[0] // 2, gains_ref[0], gains_ref[1], sums_ref, acc_ref)


def late_kernel(data_ref, gains_ref, before_ref, sums_ref, acc_ref):
    half = data_ref.shape[0] // 2
    accumulate(data_ref, half, half, gains_ref[0], gains_ref[1], sums_ref, acc_ref, before_ref)


def step_kernel(weight, data_ref, mine_ref, other_ref, gains_ref, sums_ref, new_ref, acc_ref):
    gains = gains_ref[...]
    gains = advance(gains, mine_ref[...] + other_ref[...], gains, weight)
    new_ref[...] = gains
    accumulate(data_ref, 0, data_ref.shape[0], gains[0], gains[1], sums_ref, acc_ref)


def retarget_kernel(
    weight, data_ref, mine_ref, other_ref, gains_ref, fit_ref, sums_ref, new_ref, target_ref, acc_ref
):
    consensus = by_channel(fit_ref)
    gains = gains_ref[...]
    target = consensus - (gains - consensus)
    target_ref[...] = target
    gains = advance(gains, mine_ref[...] + other_ref[...], target, weight)
    new_ref[...] = gains
    accumulate(data_ref, 0, data_ref.shape[0], gains[0], gains[1], sums_ref, acc_ref)


def by_channel(block_ref):
    pieces = [block_ref[p] for p in range(block_ref.shape[0])]
    turned = [pltpu.roll(piece, LANES - 32, 1) for piece in pieces]
    return jnp.stack([stations_in_lanes(pieces), stations_in_lanes(turned)])


def finish_kernel(weight, mine_ref, other_ref, gains_ref, target_ref, new_ref, block_ref):
    gains = advance(gains_ref[...], mine_ref[...] + other_ref[...], target_ref[...], weight)
    new_ref[...] = gains
    lane = lax.broadcasted_iota(i32, (8, LANES), 1)
    for p in range(block_ref.shape[0]):
        tile = slice(p // 4 * LANES, (p // 4 + 1) * LANES)
        shift = 32 * (p % 4)
        real = pltpu.roll(gains[0][:, tile], (LANES - shift) % LANES, 1)
        imag = pltpu.roll(gains[1][:, tile], (LANES + 32 - shift) % LANES, 1)
        block_ref[p] = jnp.where(lane < 32, real, imag)


def is_even(shape):
    return (lax.broadcasted_iota(i32, shape, 0) & 1) == 0


def basis_column(basis_ref, row, source):
    return basis_ref[row, source]


def fit_kernel(basis_ref, *refs):
    *block_refs, out_ref = refs
    even = is_even((8, LANES))
    blocks = []
    for p in range(block_refs[0].shape[0]):
        blend = block_refs[0][p]
        if len(block_refs) > 1:
            blend = blend + block_refs[1][p]
        blocks.append(blend)
    totals = []
    for row in range(4):
        total = sum(basis_column(basis_ref, row, p) * block for p, block in enumerate(blocks))
        totals.append(total + jnp.where(even, pltpu.roll(total, 7, 0), pltpu.roll(total, 1, 0)))
    lane = lax.broadcasted_iota(i32, (8, LANES), 1)
    early = jnp.where(even, totals[0], totals[1])
    late = jnp.where(even, totals[2], totals[3])
    packed = jnp.where(lane < LANES // 2, early, pltpu.roll(late, LANES // 2, 1))
    for f in range(out_ref.shape[0]):
        out_ref[f] = packed


def consensus_blocks(basis_ref, parts_ref, count):
    even = is_even((8, LANES))
    total = parts_ref[0]
    for f in range(1, parts_ref.shape[0]):
        total = total + parts_ref[f]
    rows = []
    for half in (total, pltpu.roll(total, LANES // 2, 1)):
        rows.append(jnp.where(even, half, pltpu.roll(half, 1, 0)))
        rows.append(jnp.where(even, pltpu.roll(half, 7, 0), half))
    return [
        sum(basis_column(basis_ref, row, p) * rows[row] for row in range(4)) for p in range(count)
    ]


def spread_kernel(basis_ref, parts_ref, gains_ref, out_ref, dual_ref):
    for p, block in enumerate(consensus_blocks(basis_ref, parts_ref, out_ref.shape[0])):
        out_ref[p] = block
        dual_ref[p] = gains_ref[p] - block


def write_owned(blocks, is_first, out_ref):
    owned = out_ref.shape[2]
    channels = 2 * len(blocks)
    rows = [block[2 * d : 2 * d + 2] for d in range(SKY_DIRECTIONS) for block in blocks]
    turned = jnp.concatenate(rows, 0).T
    for part in range(2):
        both = turned[part * 2 * owned : (part + 1) * 2 * owned]
        mine = jnp.where(is_first, both[:owned], both[owned:])
        for d in range(SKY_DIRECTIONS):
            out_ref[part, d] = mine[:, d * channels : (d + 1) * channels]


def place_kernel(core_ref, blocks_ref, out_ref):
    write_owned([blocks_ref[p] for p in range(blocks_ref.shape[0])], core_ref[0] == 0, out_ref)


def final_kernel(core_ref, basis_ref, parts_ref, out_ref):
    count = out_ref.shape[3] // 2
    write_owned(consensus_blocks(basis_ref, parts_ref, count), core_ref[0] == 0, out_ref)


def call(
    name, kernel, out_shape, *inputs, scalars=0, held=0, flops=0, scratch=(), limit=VMEM_LIMIT
):
    whole = pl.BlockSpec(memory_space=pltpu.VMEM)
    specs = [pl.BlockSpec(memory_space=pltpu.SMEM)] * scalars
    specs += [pl.BlockSpec(memory_space=pltpu.HBM)] * held
    specs += [whole] * (len(inputs) - len(specs))
    return pl.pallas_call(
        kernel,
        out_shape=out_shape,
        in_specs=specs,
        out_specs=jax.tree.map(lambda _: whole, out_shape),
        scratch_shapes=list(scratch),
        compiler_params=pltpu.CompilerParams(vmem_limit_bytes=limit),
        cost_estimate=pl.CostEstimate(
            flops=flops, bytes_accessed=sum(x.size * x.dtype.itemsize for x in inputs), transcendentals=0
        ),
        name=name,
    )(*inputs)


def shards(vis, coherency, gains_init, station_pairs):
    channels_dev = vis.shape[1]
    rows_dev = vis.shape[2]
    owned = gains_init.shape[3]
    pairs = lax.axis_size("pair")
    bands = lax.axis_size("freq")
    assert channels_dev == 2 * pairs and owned == 16 and STATION_TOTAL == 2 * owned * pairs
    assert ROUNDS == 2 and ITERS == 2
    weight = 2.0 * rows_dev * pairs * 2 / STATION_TOTAL
    swap = [(0, 1), (1, 0)]
    core = lax.axis_index("core").astype(i32).reshape(1)
    basis = lax.dynamic_slice_in_dim(
        jnp.asarray(basis_rows(channels_dev * bands)),
        lax.axis_index("freq") * channels_dev,
        channels_dev,
        1,
    )
    basis = basis.reshape(4, pairs, 1, 2, 1)
    basis = jnp.broadcast_to(basis, (4, pairs, SKY_DIRECTIONS, 2, LANES)).reshape(4, pairs, 8, LANES)
    shape = jax.ShapeDtypeStruct
    gains_shape = shape((2, 8, STATION_TOTAL), f32)
    sums_shape = shape((3, 8, STATION_TOTAL), f32)
    block_shape = shape((pairs, 8, LANES), f32)
    parts_shape = shape((bands, 8, LANES), f32)
    out_shape = shape((2, SKY_DIRECTIONS, owned, channels_dev), f32)
    width = 7 * rows_dev // 2 + 2 * LANES
    flops = 2 * rows_dev * pairs * 192 * 256
    scratch = [pltpu.VMEM((48 * PARTS, 2 * LANES), f32)]
    sweep = functools.partial(call, flops=flops, scratch=scratch)
    half_sweep = functools.partial(call, flops=flops // 2, scratch=scratch)

    def exchange(partial):
        return lax.ppermute(partial, "core", swap)

    def to_pairs(block):
        return lax.all_to_all(block, "pair", 0, 0, tiled=True)

    def over_bands(block):
        return lax.all_to_all(block, "freq", 0, 0, tiled=True)

    start = gains_init.transpose(0, 1, 3, 2)
    packed = call(
        "pack",
        pack_kernel,
        shape((pairs, 8, width), bf16),
        core,
        coherency,
        vis,
        station_pairs,
        start,
        exchange(start),
        scalars=1,
        held=2,
        limit=PACK_VMEM_LIMIT,
        scratch=[
            pltpu.VMEM(coherency.shape, bf16),
            pltpu.VMEM(vis.shape, f32),
            pltpu.SemaphoreType.DMA((2 * COPIES,)),
            pltpu.SemaphoreType.DMA((2 * COPIES,)),
        ],
    )
    data = to_pairs(packed)

    sums, gains = sweep("first", first_kernel, (sums_shape, gains_shape), data)
    target = gains
    sums, gains = sweep(
        "step",
        functools.partial(step_kernel, weight),
        (sums_shape, gains_shape),
        data,
        sums,
        exchange(sums),
        gains,
    )
    finish = functools.partial(finish_kernel, weight)
    gains, block = call("finish", finish, (gains_shape, block_shape), sums, exchange(sums), gains, target)
    owner_gains = to_pairs(block)
    sums = half_sweep("early", early_kernel, sums_shape, data, gains)
    owner_gains, sums = lax.optimization_barrier((owner_gains, sums))
    parts = over_bands(call("fit", fit_kernel, parts_shape, basis, owner_gains))
    sums = half_sweep("late", late_kernel, sums_shape, data, gains, sums)
    parts, sums = lax.optimization_barrier((parts, sums))
    block, owner_dual = call(
        "spread", spread_kernel, (block_shape, block_shape), basis, parts, owner_gains
    )
    fit = to_pairs(block)

    sums, gains, target = sweep(
        "retarget",
        functools.partial(retarget_kernel, weight),
        (sums_shape, gains_shape, gains_shape),
        data,
        sums,
        exchange(sums),
        gains,
        fit,
    )
    gains, block = call("finish", finish, (gains_shape, block_shape), sums, exchange(sums), gains, target)
    owner_gains = to_pairs(block)
    parts = over_bands(call("fit", fit_kernel, parts_shape, basis, owner_gains, owner_dual))
    final_gains = call("place", place_kernel, out_shape, core, owner_gains, scalars=1)
    final_consensus = call("final", final_kernel, out_shape, core, basis, parts, scalars=1)
    return (final_gains.transpose(0, 1, 3, 2), final_consensus.transpose(0, 1, 3, 2))


def solution(mesh):
    split = Mesh(
        mesh.devices.reshape(mesh.shape["freq"], mesh.shape["bl"] // 2, 2), ("freq", "pair", "core")
    )
    bl = ("pair", "core")
    placed = (
        P(None, "freq", bl),
        P(None, None, "freq", bl),
        P(None, None, "freq", bl),
        P(None, bl),
    )
    return jax.shard_map(
        shards,
        mesh=split,
        in_specs=placed,
        out_specs=(P(None, None, "freq", bl), P(None, None, "freq", bl)),
        check_vma=False,
    )
```

```python
import functools

import jax
import jax.numpy as jnp
import numpy as np
from jax import lax
from jax.experimental import pallas as pl
from jax.experimental.pallas import tpu as pltpu
from jax.sharding import Mesh, PartitionSpec as P

STATION_TOTAL = 512
SKY_DIRECTIONS = 4
ITERS = 2
ROUNDS = 2
LANES = 128
PARTS = STATION_TOTAL // LANES
UNROLL = 8
COPIES = 4
PACK_VMEM_LIMIT = 58 * 1024 * 1024
VMEM_LIMIT = 24 * 1024 * 1024
f32, bf16, i32, i16 = jnp.float32, jnp.bfloat16, jnp.int32, jnp.int16


def basis_rows(channels):
    position = (2.0 * np.arange(channels) + 1.0) / channels - 1.0
    rows = []
    for vector in [np.ones_like(position), position, position**2, position**3]:
        for other in rows:
            vector = vector - np.sum(other * vector) * other
        rows.append(vector / np.sqrt(np.sum(vector * vector)))
    return np.stack(rows).astype(np.float32)


def lanes_of(rows):
    return {"re": 0, "im": rows, "misc": 2 * rows, "low": 3 * rows, "start": 3 * rows + rows // 2}


def pick_channel_pair(by_direction, pair):
    return jnp.concatenate([block[2 * pair : 2 * pair + 2] for block in by_direction], 0)


def pack_kernel(
    coh_hbm, vis_hbm, pairs_hbm, out_hbm, coh_ref, vis_ref, pairs_ref, out_ref, coh_sem, vis_sem, pairs_sem, out_sem
):
    rows = vis_ref.shape[2]
    count = out_ref.shape[0]
    at = lanes_of(rows)
    half = rows // 2
    piece = half // COPIES
    pairs_copy = pltpu.make_async_copy(pairs_hbm, pairs_ref, pairs_sem)
    pairs_copy.start()
    copies = []
    for index in range(COPIES):
        group = []
        for side in range(2):
            lanes = pl.ds(side * half + index * piece, piece)
            slot = 2 * index + side
            group.append(
                pltpu.make_async_copy(
                    coh_hbm.at[:, :, :, lanes], coh_ref.at[:, :, :, lanes], coh_sem.at[slot]
                )
            )
            group.append(
                pltpu.make_async_copy(vis_hbm.at[:, :, lanes], vis_ref.at[:, :, lanes], vis_sem.at[slot])
            )
        for copy in group:
            copy.start()
        copies.append(group)

    def columns(index, carry):
        early = pl.multiple_of(index * LANES, LANES)
        late = pl.multiple_of(half + index * LANES, LANES)
        lower = []
        for offset in (early, late):
            lanes = pl.ds(offset, LANES)
            for part in range(2):
                blocks = [coh_ref[part, d, :, lanes].astype(f32) for d in range(SKY_DIRECTIONS)]
                place = pl.multiple_of(offset + part * rows, LANES)
                for p in range(count):
                    out_ref[p, :, pl.ds(place, LANES)] = pick_channel_pair(blocks, p).astype(bf16)
            upper = []
            for part in range(2):
                seen = vis_ref[part, :, lanes]
                rounded = seen.astype(bf16).astype(f32)
                upper.append(rounded)
                lower.append(seen - rounded)
            codes = (pairs_ref[:, lanes] - STATION_TOTAL // 2).astype(f32)
            tail = jnp.concatenate([codes, jnp.zeros((2, LANES), f32)], 0)
            place = pl.multiple_of(offset + at["misc"], LANES)
            for p in range(count):
                block = jnp.concatenate([upper[0][2 * p : 2 * p + 2], upper[1][2 * p : 2 * p + 2], tail], 0)
                out_ref[p, :, pl.ds(place, LANES)] = block.astype(bf16)
        place = pl.multiple_of(early + at["low"], LANES)
        for p in range(count):
            out_ref[p, :, pl.ds(place, LANES)] = pick_channel_pair(lower, p).astype(bf16)
        return carry

    pairs_copy.wait()
    step = piece // LANES
    sent = []
    for index, group in enumerate(copies):
        for copy in group:
            copy.wait()
        lax.fori_loop(index * step, (index + 1) * step, columns, 0)
        for start in (at["re"], at["re"] + half, at["im"], at["im"] + half, at["misc"], at["misc"] + half, at["low"]):
            lanes = pl.ds(start + index * piece, piece)
            copy = pltpu.make_async_copy(out_ref.at[:, :, lanes], out_hbm.at[:, :, lanes], out_sem.at[len(sent)])
            copy.start()
            sent.append(copy)
    for copy in sent:
        copy.wait()


def seed_kernel(core_ref, mine_ref, other_ref, packed_hbm, out_hbm, block_ref, block_sem):
    count = block_ref.shape[0]
    is_first = core_ref[0] == 0
    for part in range(2):
        mine = jnp.concatenate([mine_ref[part, d] for d in range(SKY_DIRECTIONS)], 1)
        other = jnp.concatenate([other_ref[part, d] for d in range(SKY_DIRECTIONS)], 1)
        start = jnp.concatenate([jnp.where(is_first, mine, other), jnp.where(is_first, other, mine)], 0)
        upper = start.astype(bf16).astype(f32)
        middle = (start - upper).astype(bf16).astype(f32)
        lower = start - upper - middle
        square = jnp.concatenate([upper, middle, lower, jnp.zeros_like(start)], 0).T
        blocks = [square[d * 2 * count : (d + 1) * 2 * count] for d in range(SKY_DIRECTIONS)]
        place = part * LANES
        for p in range(count):
            block_ref[p, :, place : place + LANES] = pick_channel_pair(blocks, p).astype(bf16)
    width = out_hbm.shape[2]
    copy = pltpu.make_async_copy(block_ref, out_hbm.at[:, :, width - 2 * LANES : width], block_sem)
    copy.start()
    copy.wait()


def stations_in_lanes(pieces):
    lane = lax.broadcasted_iota(i32, (8, LANES), 1)
    tiles = []
    for q in range(0, len(pieces), 4):
        tile = pieces[q]
        for k in range(1, 4):
            moved = pltpu.roll(pieces[q + k], 32 * k, 1)
            tile = jnp.where(lane >= 32 * k, moved, tile)
        tiles.append(tile)
    return jnp.concatenate(tiles, 1)


def starting_gains(data_ref):
    at = lanes_of((data_ref.shape[2] - 2 * LANES) * 2 // 7)["start"]
    parts = []
    for part in range(2):
        pieces = []
        for p in range(data_ref.shape[0]):
            piece = data_ref[p, :, at + part * LANES : at + (part + 1) * LANES].astype(f32)
            piece = piece + pltpu.roll(piece, LANES - 32, 1) + pltpu.roll(piece, LANES - 64, 1)
            pieces.append(piece)
        parts.append(stations_in_lanes(pieces))
    return parts


def lookup(words, low, high):
    picked = [jnp.take_along_axis(w, low, axis=1, mode="promise_in_bounds") for w in words]
    odd, upper = (high & 1) == 1, (high & 2) == 2
    word = jnp.where(
        upper, jnp.where(odd, picked[3], picked[2]), jnp.where(odd, picked[1], picked[0])
    )
    return (word >> 16).astype(f32), ((word & 65535) - 32768).astype(f32)


def words_of(gains_re, gains_im):
    rounded_re = gains_re.astype(bf16).astype(f32)
    rounded_im = gains_im.astype(bf16).astype(f32)
    peak = jnp.max(jnp.maximum(jnp.abs(rounded_re), jnp.abs(rounded_im)), axis=(0, 1), keepdims=True)
    unit = jnp.full((1, 1), 2.0**-60, f32)
    for power in range(-60, 60):
        unit = jnp.where(peak > 32767.0 * 2.0**power, 2.0 ** (power + 1), unit)
    inverse = 1.0 / unit
    scaled_re = jnp.round(rounded_re * inverse).astype(i32)
    scaled_im = jnp.round(rounded_im * inverse).astype(i32)
    word = (scaled_re << 16) + (scaled_im + 32768)
    return [word[:, h * LANES : (h + 1) * LANES] for h in range(PARTS)], unit


def column_terms(coh_re, coh_im, misc, low, low_row, words, square, sublane):
    def station(row):
        index = jnp.broadcast_to((misc[row : row + 1] + 256.0).astype(i32), (8, LANES))
        return index & (LANES - 1), index >> 7

    low_first, high_first = station(4)
    low_second, high_second = station(5)
    near_re, near_im = lookup(words, low_first, high_first)
    far_re, far_im = lookup(words, low_second, high_second)
    z_re = coh_re * far_re + coh_im * far_im
    z_im = coh_im * far_re - coh_re * far_im
    x_re = near_re * coh_re - near_im * coh_im
    x_im = near_re * coh_im + near_im * coh_re
    inside = lambda row: (sublane >= row) & (sublane < row + 2)
    vis_re = jnp.where(inside(0), misc, jnp.where(inside(low_row), low, 0.0))
    vis_im = jnp.where(inside(2), misc, jnp.where(inside(low_row + 2), low, 0.0))
    if low_row == 0:
        vis_re = jnp.where(inside(0), misc + low, 0.0)
        vis_im = jnp.where(inside(2), misc + low, 0.0)
    res_re = vis_re - square * (near_re * z_re - near_im * z_im)
    res_im = vis_im - square * (near_re * z_im + near_im * z_re)
    res_re = res_re + pltpu.roll(res_re, 4, 0)
    res_re = res_re + pltpu.roll(res_re, 2, 0)
    res_im = res_im + pltpu.roll(res_im, 4, 0)
    res_im = res_im + pltpu.roll(res_im, 2, 0)
    first = jnp.concatenate([res_re * z_re + res_im * z_im, res_im * z_re - res_re * z_im], 0)
    second = jnp.concatenate([res_re * x_re + res_im * x_im, res_re * x_im - res_im * x_re], 0)
    first_norm = z_re * z_re + z_im * z_im
    second_norm = x_re * x_re + x_im * x_im
    twice = lambda a: jnp.concatenate([a, a], 0).astype(bf16)
    return (
        (first.astype(bf16), twice(first_norm), low_first, high_first),
        (second.astype(bf16), twice(second_norm), low_second, high_second),
    )


def operands(term, station_rows, half_rows):
    pair, norm, low, high = term
    zero = jnp.zeros_like(pair)
    high = jnp.broadcast_to(high[:1], (16, LANES)).astype(i16)
    rows = [jnp.where(high == i16(h), pair, zero) for h in range(PARTS)]
    rows += [jnp.where(high == half_rows + i16(h), norm, zero) for h in range(0, PARTS, 2)]
    low = jnp.broadcast_to(low[:1].astype(f32), (LANES, LANES)).astype(bf16)
    table = jnp.where(station_rows == low, jnp.ones_like(low), jnp.zeros_like(low))
    return jnp.concatenate(rows, 0), table


def accumulate(data_ref, first, count, gains_re, gains_im, sums_ref, acc_ref, before=None):
    rows = (data_ref.shape[2] - 2 * LANES) * 2 // 7
    at = lanes_of(rows)
    half = rows // 2
    words, unit = words_of(gains_re, gains_im)
    square = jnp.broadcast_to(unit * unit, (8, LANES))
    station_rows = lax.broadcasted_iota(i32, (LANES, LANES), 0).astype(f32).astype(bf16)
    half_rows = (lax.broadcasted_iota(i32, (16, LANES), 0) >> 3).astype(i16)
    sublane = lax.broadcasted_iota(i32, (8, LANES), 0)
    acc_ref[...] = jnp.zeros_like(acc_ref)

    def step(source, carry):
        left, right = [], []
        for offset in range(0, rows, LANES):
            load = lambda start: data_ref[source, :, start : start + LANES].astype(f32)
            low = load(at["low"] + offset % half)
            terms = column_terms(
                load(at["re"] + offset),
                load(at["im"] + offset),
                load(at["misc"] + offset),
                low,
                4 * (offset // half),
                words,
                square,
                sublane,
            )
            (rows_first, table_first), (rows_second, table_second) = [
                operands(term, station_rows, half_rows) for term in terms
            ]
            left.append(jnp.concatenate([rows_first, rows_second], 0))
            right.append(jnp.concatenate([table_first, table_second], 0))
        acc_ref[...] += lax.dot_general(
            jnp.concatenate(right, 1),
            jnp.concatenate(left, 1),
            (((1,), (1,)), ((), ())),
            preferred_element_type=f32,
        )
        return carry

    lax.fori_loop(first, first + count, step, 0, unroll=UNROLL)
    tall = 24 * PARTS
    acc = (acc_ref[0:LANES, 0:tall] + acc_ref[LANES : 2 * LANES, tall : 2 * tall]).T
    base = 16 * PARTS
    sums = [
        jnp.concatenate([acc[16 * h : 16 * h + 8] for h in range(PARTS)], 1),
        jnp.concatenate([acc[16 * h + 8 : 16 * h + 16] for h in range(PARTS)], 1),
        jnp.concatenate([acc[base + 8 * h : base + 8 * h + 8] for h in range(PARTS)], 1),
    ]
    for k, factor in enumerate((unit, unit, unit * unit)):
        part = sums[k] * factor
        sums_ref[k] = part if before is None else before[k] + part


def advance(gains, sums, target, penalty_weight):
    return gains + (sums[0:2] + penalty_weight * (target - gains)) / (
        2.0 * sums[2] + penalty_weight
    )


def first_kernel(data_ref, sums_ref, gains_ref, acc_ref):
    gains = starting_gains(data_ref)
    gains_ref[0], gains_ref[1] = gains
    accumulate(data_ref, 0, data_ref.shape[0], *gains, sums_ref, acc_ref)


def early_kernel(data_ref, gains_ref, sums_ref, acc_ref):
    accumulate(data_ref, 0, data_ref.shape[0] // 2, gains_ref[0], gains_ref[1], sums_ref, acc_ref)


def late_kernel(data_ref, gains_ref, before_ref, sums_ref, acc_ref):
    half = data_ref.shape[0] // 2
    accumulate(data_ref, half, half, gains_ref[0], gains_ref[1], sums_ref, acc_ref, before_ref)


def step_kernel(weight, data_ref, mine_ref, other_ref, gains_ref, sums_ref, new_ref, acc_ref):
    gains = gains_ref[...]
    gains = advance(gains, mine_ref[...] + other_ref[...], gains, weight)
    new_ref[...] = gains
    accumulate(data_ref, 0, data_ref.shape[0], gains[0], gains[1], sums_ref, acc_ref)


def retarget_kernel(
    weight, data_ref, mine_ref, other_ref, gains_ref, fit_ref, sums_ref, new_ref, target_ref, acc_ref
):
    consensus = by_channel(fit_ref)
    gains = gains_ref[...]
    target = consensus - (gains - consensus)
    target_ref[...] = target
    gains = advance(gains, mine_ref[...] + other_ref[...], target, weight)
    new_ref[...] = gains
    accumulate(data_ref, 0, data_ref.shape[0], gains[0], gains[1], sums_ref, acc_ref)


def by_channel(block_ref):
    pieces = [block_ref[p] for p in range(block_ref.shape[0])]
    turned = [pltpu.roll(piece, LANES - 32, 1) for piece in pieces]
    return jnp.stack([stations_in_lanes(pieces), stations_in_lanes(turned)])


def finish_kernel(weight, mine_ref, other_ref, gains_ref, target_ref, new_ref, block_ref):
    gains = advance(gains_ref[...], mine_ref[...] + other_ref[...], target_ref[...], weight)
    new_ref[...] = gains
    lane = lax.broadcasted_iota(i32, (8, LANES), 1)
    for p in range(block_ref.shape[0]):
        tile = slice(p // 4 * LANES, (p // 4 + 1) * LANES)
        shift = 32 * (p % 4)
        real = pltpu.roll(gains[0][:, tile], (LANES - shift) % LANES, 1)
        imag = pltpu.roll(gains[1][:, tile], (LANES + 32 - shift) % LANES, 1)
        block_ref[p] = jnp.where(lane < 32, real, imag)


def is_even(shape):
    return (lax.broadcasted_iota(i32, shape, 0) & 1) == 0


def basis_column(basis_ref, row, source):
    return basis_ref[row, source]


def fit_kernel(basis_ref, *refs):
    *block_refs, out_ref = refs
    even = is_even((8, LANES))
    blocks = []
    for p in range(block_refs[0].shape[0]):
        blend = block_refs[0][p]
        if len(block_refs) > 1:
            blend = blend + block_refs[1][p]
        blocks.append(blend)
    totals = []
    for row in range(4):
        total = sum(basis_column(basis_ref, row, p) * block for p, block in enumerate(blocks))
        totals.append(total + jnp.where(even, pltpu.roll(total, 7, 0), pltpu.roll(total, 1, 0)))
    lane = lax.broadcasted_iota(i32, (8, LANES), 1)
    early = jnp.where(even, totals[0], totals[1])
    late = jnp.where(even, totals[2], totals[3])
    packed = jnp.where(lane < LANES // 2, early, pltpu.roll(late, LANES // 2, 1))
    for f in range(out_ref.shape[0]):
        out_ref[f] = packed


def consensus_blocks(basis_ref, parts_ref, count):
    even = is_even((8, LANES))
    total = parts_ref[0]
    for f in range(1, parts_ref.shape[0]):
        total = total + parts_ref[f]
    rows = []
    for half in (total, pltpu.roll(total, LANES // 2, 1)):
        rows.append(jnp.where(even, half, pltpu.roll(half, 1, 0)))
        rows.append(jnp.where(even, pltpu.roll(half, 7, 0), half))
    return [
        sum(basis_column(basis_ref, row, p) * rows[row] for row in range(4)) for p in range(count)
    ]


def spread_kernel(basis_ref, parts_ref, gains_ref, out_ref, dual_ref):
    for p, block in enumerate(consensus_blocks(basis_ref, parts_ref, out_ref.shape[0])):
        out_ref[p] = block
        dual_ref[p] = gains_ref[p] - block


def write_owned(blocks, is_first, out_ref):
    owned = out_ref.shape[2]
    channels = 2 * len(blocks)
    rows = [block[2 * d : 2 * d + 2] for d in range(SKY_DIRECTIONS) for block in blocks]
    turned = jnp.concatenate(rows, 0).T
    for part in range(2):
        both = turned[part * 2 * owned : (part + 1) * 2 * owned]
        mine = jnp.where(is_first, both[:owned], both[owned:])
        for d in range(SKY_DIRECTIONS):
            out_ref[part, d] = mine[:, d * channels : (d + 1) * channels]


def place_kernel(core_ref, blocks_ref, out_ref):
    write_owned([blocks_ref[p] for p in range(blocks_ref.shape[0])], core_ref[0] == 0, out_ref)


def final_kernel(core_ref, basis_ref, parts_ref, out_ref):
    count = out_ref.shape[3] // 2
    write_owned(consensus_blocks(basis_ref, parts_ref, count), core_ref[0] == 0, out_ref)


def call(
    name,
    kernel,
    out_shape,
    *inputs,
    scalars=0,
    in_hbm=(),
    out_hbm=False,
    aliases=None,
    flops=0,
    scratch=(),
    limit=VMEM_LIMIT,
):
    whole = pl.BlockSpec(memory_space=pltpu.VMEM)
    outside = pl.BlockSpec(memory_space=pltpu.HBM)
    specs = [pl.BlockSpec(memory_space=pltpu.SMEM)] * scalars
    specs += [outside if k in in_hbm else whole for k in range(scalars, len(inputs))]
    return pl.pallas_call(
        kernel,
        out_shape=out_shape,
        in_specs=specs,
        out_specs=jax.tree.map(lambda _: outside if out_hbm else whole, out_shape),
        scratch_shapes=list(scratch),
        input_output_aliases=aliases or {},
        compiler_params=pltpu.CompilerParams(vmem_limit_bytes=limit),
        cost_estimate=pl.CostEstimate(
            flops=flops, bytes_accessed=sum(x.size * x.dtype.itemsize for x in inputs), transcendentals=0
        ),
        name=name,
    )(*inputs)


def shards(vis, coherency, gains_init, station_pairs):
    channels_dev = vis.shape[1]
    rows_dev = vis.shape[2]
    owned = gains_init.shape[3]
    pairs = lax.axis_size("pair")
    bands = lax.axis_size("freq")
    assert channels_dev == 2 * pairs and owned == 16 and STATION_TOTAL == 2 * owned * pairs
    assert ROUNDS == 2 and ITERS == 2
    weight = 2.0 * rows_dev * pairs * 2 / STATION_TOTAL
    swap = [(0, 1), (1, 0)]
    core = lax.axis_index("core").astype(i32).reshape(1)
    basis = lax.dynamic_slice_in_dim(
        jnp.asarray(basis_rows(channels_dev * bands)),
        lax.axis_index("freq") * channels_dev,
        channels_dev,
        1,
    )
    basis = basis.reshape(4, pairs, 1, 2, 1)
    basis = jnp.broadcast_to(basis, (4, pairs, SKY_DIRECTIONS, 2, LANES)).reshape(4, pairs, 8, LANES)
    shape = jax.ShapeDtypeStruct
    gains_shape = shape((2, 8, STATION_TOTAL), f32)
    sums_shape = shape((3, 8, STATION_TOTAL), f32)
    block_shape = shape((pairs, 8, LANES), f32)
    parts_shape = shape((bands, 8, LANES), f32)
    out_shape = shape((2, SKY_DIRECTIONS, owned, channels_dev), f32)
    width = 7 * rows_dev // 2 + 2 * LANES
    flops = 2 * rows_dev * pairs * 192 * 256
    scratch = [pltpu.VMEM((2 * LANES, 48 * PARTS), f32)]
    sweep = functools.partial(call, flops=flops, scratch=scratch)
    half_sweep = functools.partial(call, flops=flops // 2, scratch=scratch)

    def exchange(partial):
        return lax.ppermute(partial, "core", swap)

    def to_pairs(block):
        return lax.all_to_all(block, "pair", 0, 0, tiled=True)

    def over_bands(block):
        return lax.all_to_all(block, "freq", 0, 0, tiled=True)

    start = gains_init.transpose(0, 1, 3, 2)
    packed_shape = shape((pairs, 8, width), bf16)
    packed = call(
        "pack",
        pack_kernel,
        packed_shape,
        coherency,
        vis,
        station_pairs,
        in_hbm=(0, 1, 2),
        out_hbm=True,
        limit=PACK_VMEM_LIMIT,
        scratch=[
            pltpu.VMEM(coherency.shape, bf16),
            pltpu.VMEM(vis.shape, f32),
            pltpu.VMEM(station_pairs.shape, i32),
            pltpu.VMEM(packed_shape.shape, bf16),
            pltpu.SemaphoreType.DMA((2 * COPIES,)),
            pltpu.SemaphoreType.DMA((2 * COPIES,)),
            pltpu.SemaphoreType.DMA,
            pltpu.SemaphoreType.DMA((7 * COPIES,)),
        ],
    )
    packed = call(
        "seed",
        seed_kernel,
        packed_shape,
        core,
        start,
        exchange(start),
        packed,
        scalars=1,
        in_hbm=(3,),
        out_hbm=True,
        aliases={3: 0},
        limit=PACK_VMEM_LIMIT,
        scratch=[pltpu.VMEM((pairs, 8, 2 * LANES), bf16), pltpu.SemaphoreType.DMA],
    )
    data = to_pairs(packed)

    sums, gains = sweep("first", first_kernel, (sums_shape, gains_shape), data)
    target = gains
    sums, gains = sweep(
        "step",
        functools.partial(step_kernel, weight),
        (sums_shape, gains_shape),
        data,
        sums,
        exchange(sums),
        gains,
    )
    finish = functools.partial(finish_kernel, weight)
    gains, block = call("finish", finish, (gains_shape, block_shape), sums, exchange(sums), gains, target)
    owner_gains = to_pairs(block)
    sums = half_sweep("early", early_kernel, sums_shape, data, gains)
    owner_gains, sums = lax.optimization_barrier((owner_gains, sums))
    parts = over_bands(call("fit", fit_kernel, parts_shape, basis, owner_gains))
    sums = half_sweep("late", late_kernel, sums_shape, data, gains, sums)
    parts, sums = lax.optimization_barrier((parts, sums))
    block, owner_dual = call(
        "spread", spread_kernel, (block_shape, block_shape), basis, parts, owner_gains
    )
    fit = to_pairs(block)

    sums, gains, target = sweep(
        "retarget",
        functools.partial(retarget_kernel, weight),
        (sums_shape, gains_shape, gains_shape),
        data,
        sums,
        exchange(sums),
        gains,
        fit,
    )
    gains, block = call("finish", finish, (gains_shape, block_shape), sums, exchange(sums), gains, target)
    owner_gains = to_pairs(block)
    parts = over_bands(call("fit", fit_kernel, parts_shape, basis, owner_gains, owner_dual))
    final_gains = call("place", place_kernel, out_shape, core, owner_gains, scalars=1)
    final_consensus = call("final", final_kernel, out_shape, core, basis, parts, scalars=1)
    return (final_gains.transpose(0, 1, 3, 2), final_consensus.transpose(0, 1, 3, 2))


def solution(mesh):
    split = Mesh(
        mesh.devices.reshape(mesh.shape["freq"], mesh.shape["bl"] // 2, 2), ("freq", "pair", "core")
    )
    bl = ("pair", "core")
    placed = (
        P(None, "freq", bl),
        P(None, None, "freq", bl),
        P(None, None, "freq", bl),
        P(None, bl),
    )
    return jax.shard_map(
        shards,
        mesh=split,
        in_specs=placed,
        out_specs=(P(None, None, "freq", bl), P(None, None, "freq", bl)),
        check_vma=False,
    )
```

```python
import functools

import jax
import jax.numpy as jnp
import numpy as np
from jax import lax
from jax.experimental import pallas as pl
from jax.experimental.pallas import tpu as pltpu
from jax.sharding import Mesh, PartitionSpec as P

STATION_TOTAL = 512
SKY_DIRECTIONS = 4
ITERS = 2
ROUNDS = 2
LANES = 128
PARTS = STATION_TOTAL // LANES
UNROLL = 8
COH_STEPS = 4096.0
GAIN_STEPS = 4096.0
REST_STEPS = 2.0**27
COPIES = 4
PACK_VMEM_LIMIT = 58 * 1024 * 1024
SEED_VMEM_LIMIT = 53 * 1024 * 1024
VMEM_LIMIT = 24 * 1024 * 1024
f32, bf16, i32, i16 = jnp.float32, jnp.bfloat16, jnp.int32, jnp.int16


def basis_rows(channels):
    position = (2.0 * np.arange(channels) + 1.0) / channels - 1.0
    rows = []
    for vector in [np.ones_like(position), position, position**2, position**3]:
        for other in rows:
            vector = vector - np.sum(other * vector) * other
        rows.append(vector / np.sqrt(np.sum(vector * vector)))
    return np.stack(rows).astype(np.float32)


def lanes_of(rows):
    return {"re": 0, "im": rows, "misc": 2 * rows, "start": 3 * rows}


def rows_of(data_ref):
    return (data_ref.shape[2] - LANES) // 3


def coded(values):
    return jnp.round(values).astype(i32).astype(i16)


def pick_channel_pair(by_direction, pair):
    return jnp.concatenate([block[2 * pair : 2 * pair + 2] for block in by_direction], 0)


def pack_kernel(
    coh_hbm, vis_hbm, pairs_hbm, out_hbm, coh_ref, vis_ref, pairs_ref, out_ref, coh_sem, vis_sem, pairs_sem, out_sem
):
    rows = vis_ref.shape[2]
    count = out_ref.shape[0]
    channels = vis_ref.shape[1]
    at = lanes_of(rows)
    half = rows // 2
    piece = half // COPIES
    pairs_copy = pltpu.make_async_copy(pairs_hbm, pairs_ref, pairs_sem)
    pairs_copy.start()
    copies = []
    for index in range(COPIES):
        group = []
        for side in range(2):
            lanes = pl.ds(side * half + index * piece, piece)
            slot = 2 * index + side
            group.append(
                pltpu.make_async_copy(
                    coh_hbm.at[:, :, :, lanes], coh_ref.at[:, :, :, lanes], coh_sem.at[slot]
                )
            )
            group.append(
                pltpu.make_async_copy(vis_hbm.at[:, :, lanes], vis_ref.at[:, :, lanes], vis_sem.at[slot])
            )
        copies.append(group)
    for kind in (1, 0):
        for group in copies:
            for copy in group[kind::2]:
                copy.start()
    for group in copies:
        for copy in group[1::2]:
            copy.wait()
    peak = jnp.zeros((channels, LANES), f32)
    for start in range(0, rows, LANES):
        for part in range(2):
            peak = jnp.maximum(peak, jnp.abs(vis_ref[part, :, start : start + LANES]))
    peak = jnp.max(peak, axis=(0, 1), keepdims=True)
    exponent = jnp.full((1, 1), -60.0, f32)
    inverse = jnp.full((1, 1), 2.0**60, f32)
    for power in range(-60, -8):
        over = peak > 32767.0 * 2.0**power
        exponent = jnp.where(over, power + 1.0, exponent)
        inverse = jnp.where(over, 2.0 ** (-power - 1), inverse)
    exponent = jnp.broadcast_to(exponent, (2, LANES))

    def columns(index, carry):
        early = pl.multiple_of(index * LANES, LANES)
        late = pl.multiple_of(half + index * LANES, LANES)
        for offset in (early, late):
            lanes = pl.ds(offset, LANES)
            for part in range(2):
                blocks = [coh_ref[part, d, :, lanes].astype(f32) * COH_STEPS for d in range(SKY_DIRECTIONS)]
                place = pl.multiple_of(offset + part * rows, LANES)
                for p in range(count):
                    out_ref[p, :, pl.ds(place, LANES)] = coded(pick_channel_pair(blocks, p))
            seen = [vis_ref[part, :, lanes] * inverse for part in range(2)]
            tail = jnp.concatenate([pairs_ref[:, lanes].astype(f32), exponent], 0)
            place = pl.multiple_of(offset + at["misc"], LANES)
            for p in range(count):
                block = jnp.concatenate([seen[0][2 * p : 2 * p + 2], seen[1][2 * p : 2 * p + 2], tail], 0)
                out_ref[p, :, pl.ds(place, LANES)] = coded(block)
        return carry

    pairs_copy.wait()
    step = piece // LANES
    sent = []
    for index, group in enumerate(copies):
        for copy in group[0::2]:
            copy.wait()
        lax.fori_loop(index * step, (index + 1) * step, columns, 0)
        for start in (at["re"], at["re"] + half, at["im"], at["im"] + half, at["misc"], at["misc"] + half):
            lanes = pl.ds(start + index * piece, piece)
            copy = pltpu.make_async_copy(out_ref.at[:, :, lanes], out_hbm.at[:, :, lanes], out_sem.at[len(sent)])
            copy.start()
            sent.append(copy)
    for copy in sent:
        copy.wait()


def seed_kernel(core_ref, mine_ref, other_ref, packed_hbm, out_hbm, block_ref, block_sem):
    count = block_ref.shape[0]
    is_first = core_ref[0] == 0
    parts = []
    for part in range(2):
        mine = jnp.concatenate([mine_ref[part, d] for d in range(SKY_DIRECTIONS)], 1)
        other = jnp.concatenate([other_ref[part, d] for d in range(SKY_DIRECTIONS)], 1)
        start = jnp.concatenate([jnp.where(is_first, mine, other), jnp.where(is_first, other, mine)], 0)
        coarse = jnp.round(start * GAIN_STEPS)
        parts += [coarse, jnp.round((start - coarse * (1.0 / GAIN_STEPS)) * REST_STEPS)]
    square = jnp.concatenate(parts, 0).T
    blocks = [square[d * 2 * count : (d + 1) * 2 * count] for d in range(SKY_DIRECTIONS)]
    for p in range(count):
        block_ref[p] = coded(pick_channel_pair(blocks, p))
    width = out_hbm.shape[2]
    copy = pltpu.make_async_copy(block_ref, out_hbm.at[:, :, width - LANES : width], block_sem)
    copy.start()
    copy.wait()


def stations_in_lanes(pieces):
    lane = lax.broadcasted_iota(i32, (8, LANES), 1)
    tiles = []
    for q in range(0, len(pieces), 4):
        tile = pieces[q]
        for k in range(1, 4):
            moved = pltpu.roll(pieces[q + k], 32 * k, 1)
            tile = jnp.where(lane >= 32 * k, moved, tile)
        tiles.append(tile)
    return jnp.concatenate(tiles, 1)


def starting_gains(data_ref):
    at = lanes_of(rows_of(data_ref))["start"]
    parts = []
    for part in range(2):
        pieces = []
        for p in range(data_ref.shape[0]):
            piece = data_ref[p, :, at : at + LANES].astype(i32).astype(f32)
            if part:
                piece = pltpu.roll(piece, LANES - 64, 1)
            piece = piece * (1.0 / GAIN_STEPS) + pltpu.roll(piece, LANES - 32, 1) * (1.0 / REST_STEPS)
            pieces.append(piece)
        parts.append(stations_in_lanes(pieces))
    return parts


def lookup(words, low, high):
    picked = [jnp.take_along_axis(w, low, axis=1, mode="promise_in_bounds") for w in words]
    odd, upper = (high & 1) == 1, (high & 2) == 2
    word = jnp.where(
        upper, jnp.where(odd, picked[3], picked[2]), jnp.where(odd, picked[1], picked[0])
    )
    return (word >> 16).astype(f32), ((word & 65535) - 32768).astype(f32)


def words_of(gains_re, gains_im):
    rounded_re = gains_re.astype(bf16).astype(f32)
    rounded_im = gains_im.astype(bf16).astype(f32)
    peak = jnp.max(jnp.maximum(jnp.abs(rounded_re), jnp.abs(rounded_im)), axis=(0, 1), keepdims=True)
    unit = jnp.full((1, 1), 2.0**-60, f32)
    for power in range(-60, 60):
        unit = jnp.where(peak > 32767.0 * 2.0**power, 2.0 ** (power + 1), unit)
    inverse = 1.0 / unit
    scaled_re = jnp.round(rounded_re * inverse).astype(i32)
    scaled_im = jnp.round(rounded_im * inverse).astype(i32)
    word = (scaled_re << 16) + (scaled_im + 32768)
    return [word[:, h * LANES : (h + 1) * LANES] for h in range(PARTS)], unit


def column_terms(coh_re, coh_im, misc, vis_unit, words, square, sublane):
    def station(row):
        index = jnp.broadcast_to(misc[row : row + 1], (8, LANES))
        return index & (LANES - 1), index >> 7

    low_first, high_first = station(4)
    low_second, high_second = station(5)
    near_re, near_im = lookup(words, low_first, high_first)
    far_re, far_im = lookup(words, low_second, high_second)
    z_re = coh_re * far_re + coh_im * far_im
    z_im = coh_im * far_re - coh_re * far_im
    x_re = near_re * coh_re - near_im * coh_im
    x_im = near_re * coh_im + near_im * coh_re
    seen = misc.astype(f32) * vis_unit
    vis_re = jnp.where(sublane < 2, seen, 0.0)
    vis_im = jnp.where((sublane >= 2) & (sublane < 4), seen, 0.0)
    res_re = vis_re - square * (near_re * z_re - near_im * z_im)
    res_im = vis_im - square * (near_re * z_im + near_im * z_re)
    res_re = res_re + pltpu.roll(res_re, 4, 0)
    res_re = res_re + pltpu.roll(res_re, 2, 0)
    res_im = res_im + pltpu.roll(res_im, 4, 0)
    res_im = res_im + pltpu.roll(res_im, 2, 0)
    first = jnp.concatenate([res_re * z_re + res_im * z_im, res_im * z_re - res_re * z_im], 0)
    second = jnp.concatenate([res_re * x_re + res_im * x_im, res_re * x_im - res_im * x_re], 0)
    first_norm = z_re * z_re + z_im * z_im
    second_norm = x_re * x_re + x_im * x_im
    twice = lambda a: jnp.concatenate([a, a], 0).astype(bf16)
    return (
        (first.astype(bf16), twice(first_norm), low_first, high_first),
        (second.astype(bf16), twice(second_norm), low_second, high_second),
    )


def operands(term, station_rows, half_rows):
    pair, norm, low, high = term
    zero = jnp.zeros_like(pair)
    high = jnp.broadcast_to(high[:1], (16, LANES)).astype(i16)
    rows = [jnp.where(high == i16(h), pair, zero) for h in range(PARTS)]
    rows += [jnp.where(high == half_rows + i16(h), norm, zero) for h in range(0, PARTS, 2)]
    low = jnp.broadcast_to(low[:1].astype(f32), (LANES, LANES)).astype(bf16)
    table = jnp.where(station_rows == low, jnp.ones_like(low), jnp.zeros_like(low))
    return jnp.concatenate(rows, 0), table


def accumulate(data_ref, first, count, gains_re, gains_im, sums_ref, acc_ref, before=None):
    rows = rows_of(data_ref)
    at = lanes_of(rows)
    words, unit = words_of(gains_re, gains_im)
    square = jnp.broadcast_to(unit * unit * (1.0 / COH_STEPS), (8, LANES))
    unit = unit * (1.0 / COH_STEPS)
    station_rows = lax.broadcasted_iota(i32, (LANES, LANES), 0).astype(f32).astype(bf16)
    half_rows = (lax.broadcasted_iota(i32, (16, LANES), 0) >> 3).astype(i16)
    sublane = lax.broadcasted_iota(i32, (8, LANES), 0)
    acc_ref[...] = jnp.zeros_like(acc_ref)

    def step(source, carry):
        left, right = [], []
        exponent = data_ref[source, :, at["misc"] : at["misc"] + LANES].astype(i32).astype(f32)
        vis_unit = jnp.exp2(jnp.broadcast_to(exponent[6:7], (8, LANES)))
        for offset in range(0, rows, LANES):
            load = lambda start: data_ref[source, :, start : start + LANES].astype(i32)
            terms = column_terms(
                load(at["re"] + offset).astype(f32),
                load(at["im"] + offset).astype(f32),
                load(at["misc"] + offset),
                vis_unit,
                words,
                square,
                sublane,
            )
            (rows_first, table_first), (rows_second, table_second) = [
                operands(term, station_rows, half_rows) for term in terms
            ]
            left.append(jnp.concatenate([rows_first, rows_second], 0))
            right.append(jnp.concatenate([table_first, table_second], 0))
        acc_ref[...] += lax.dot_general(
            jnp.concatenate(right, 1),
            jnp.concatenate(left, 1),
            (((1,), (1,)), ((), ())),
            preferred_element_type=f32,
        )
        return carry

    lax.fori_loop(first, first + count, step, 0, unroll=UNROLL)
    tall = 24 * PARTS
    acc = (acc_ref[0:LANES, 0:tall] + acc_ref[LANES : 2 * LANES, tall : 2 * tall]).T
    base = 16 * PARTS
    sums = [
        jnp.concatenate([acc[16 * h : 16 * h + 8] for h in range(PARTS)], 1),
        jnp.concatenate([acc[16 * h + 8 : 16 * h + 16] for h in range(PARTS)], 1),
        jnp.concatenate([acc[base + 8 * h : base + 8 * h + 8] for h in range(PARTS)], 1),
    ]
    for k, factor in enumerate((unit, unit, unit * unit)):
        part = sums[k] * factor
        sums_ref[k] = part if before is None else before[k] + part


def advance(gains, sums, target, penalty_weight):
    return gains + (sums[0:2] + penalty_weight * (target - gains)) / (
        2.0 * sums[2] + penalty_weight
    )


def first_kernel(data_ref, sums_ref, gains_ref, acc_ref):
    gains = starting_gains(data_ref)
    gains_ref[0], gains_ref[1] = gains
    accumulate(data_ref, 0, data_ref.shape[0], *gains, sums_ref, acc_ref)


def early_kernel(data_ref, gains_ref, sums_ref, acc_ref):
    accumulate(data_ref, 0, data_ref.shape[0] // 2, gains_ref[0], gains_ref[1], sums_ref, acc_ref)


def late_kernel(data_ref, gains_ref, before_ref, sums_ref, acc_ref):
    half = data_ref.shape[0] // 2
    accumulate(data_ref, half, half, gains_ref[0], gains_ref[1], sums_ref, acc_ref, before_ref)


def step_kernel(weight, data_ref, mine_ref, other_ref, gains_ref, sums_ref, new_ref, acc_ref):
    gains = gains_ref[...]
    gains = advance(gains, mine_ref[...] + other_ref[...], gains, weight)
    new_ref[...] = gains
    accumulate(data_ref, 0, data_ref.shape[0], gains[0], gains[1], sums_ref, acc_ref)


def retarget_kernel(
    weight, data_ref, mine_ref, other_ref, gains_ref, fit_ref, sums_ref, new_ref, target_ref, acc_ref
):
    consensus = by_channel(fit_ref)
    gains = gains_ref[...]
    target = consensus - (gains - consensus)
    target_ref[...] = target
    gains = advance(gains, mine_ref[...] + other_ref[...], target, weight)
    new_ref[...] = gains
    accumulate(data_ref, 0, data_ref.shape[0], gains[0], gains[1], sums_ref, acc_ref)


def by_channel(block_ref):
    pieces = [block_ref[p] for p in range(block_ref.shape[0])]
    turned = [pltpu.roll(piece, LANES - 32, 1) for piece in pieces]
    return jnp.stack([stations_in_lanes(pieces), stations_in_lanes(turned)])


def finish_kernel(weight, mine_ref, other_ref, gains_ref, target_ref, new_ref, block_ref):
    gains = advance(gains_ref[...], mine_ref[...] + other_ref[...], target_ref[...], weight)
    new_ref[...] = gains
    lane = lax.broadcasted_iota(i32, (8, LANES), 1)
    for p in range(block_ref.shape[0]):
        tile = slice(p // 4 * LANES, (p // 4 + 1) * LANES)
        shift = 32 * (p % 4)
        real = pltpu.roll(gains[0][:, tile], (LANES - shift) % LANES, 1)
        imag = pltpu.roll(gains[1][:, tile], (LANES + 32 - shift) % LANES, 1)
        block_ref[p] = jnp.where(lane < 32, real, imag)


def is_even(shape):
    return (lax.broadcasted_iota(i32, shape, 0) & 1) == 0


def basis_column(basis_ref, row, source):
    return basis_ref[row, source]


def fit_kernel(basis_ref, *refs):
    *block_refs, out_ref = refs
    even = is_even((8, LANES))
    blocks = []
    for p in range(block_refs[0].shape[0]):
        blend = block_refs[0][p]
        if len(block_refs) > 1:
            blend = blend + block_refs[1][p]
        blocks.append(blend)
    totals = []
    for row in range(4):
        total = sum(basis_column(basis_ref, row, p) * block for p, block in enumerate(blocks))
        totals.append(total + jnp.where(even, pltpu.roll(total, 7, 0), pltpu.roll(total, 1, 0)))
    lane = lax.broadcasted_iota(i32, (8, LANES), 1)
    early = jnp.where(even, totals[0], totals[1])
    late = jnp.where(even, totals[2], totals[3])
    packed = jnp.where(lane < LANES // 2, early, pltpu.roll(late, LANES // 2, 1))
    for f in range(out_ref.shape[0]):
        out_ref[f] = packed


def consensus_blocks(basis_ref, parts_ref, count):
    even = is_even((8, LANES))
    total = parts_ref[0]
    for f in range(1, parts_ref.shape[0]):
        total = total + parts_ref[f]
    rows = []
    for half in (total, pltpu.roll(total, LANES // 2, 1)):
        rows.append(jnp.where(even, half, pltpu.roll(half, 1, 0)))
        rows.append(jnp.where(even, pltpu.roll(half, 7, 0), half))
    return [
        sum(basis_column(basis_ref, row, p) * rows[row] for row in range(4)) for p in range(count)
    ]


def spread_kernel(basis_ref, parts_ref, gains_ref, out_ref, dual_ref):
    for p, block in enumerate(consensus_blocks(basis_ref, parts_ref, out_ref.shape[0])):
        out_ref[p] = block
        dual_ref[p] = gains_ref[p] - block


def write_owned(blocks, is_first, out_ref):
    owned = out_ref.shape[2]
    channels = 2 * len(blocks)
    rows = [block[2 * d : 2 * d + 2] for d in range(SKY_DIRECTIONS) for block in blocks]
    turned = jnp.concatenate(rows, 0).T
    for part in range(2):
        both = turned[part * 2 * owned : (part + 1) * 2 * owned]
        mine = jnp.where(is_first, both[:owned], both[owned:])
        for d in range(SKY_DIRECTIONS):
            out_ref[part, d] = mine[:, d * channels : (d + 1) * channels]


def place_kernel(core_ref, blocks_ref, out_ref):
    write_owned([blocks_ref[p] for p in range(blocks_ref.shape[0])], core_ref[0] == 0, out_ref)


def final_kernel(core_ref, basis_ref, parts_ref, out_ref):
    count = out_ref.shape[3] // 2
    write_owned(consensus_blocks(basis_ref, parts_ref, count), core_ref[0] == 0, out_ref)


def call(
    name,
    kernel,
    out_shape,
    *inputs,
    scalars=0,
    in_hbm=(),
    out_hbm=False,
    aliases=None,
    flops=0,
    scratch=(),
    limit=VMEM_LIMIT,
):
    whole = pl.BlockSpec(memory_space=pltpu.VMEM)
    outside = pl.BlockSpec(memory_space=pltpu.HBM)
    specs = [pl.BlockSpec(memory_space=pltpu.SMEM)] * scalars
    specs += [outside if k in in_hbm else whole for k in range(scalars, len(inputs))]
    return pl.pallas_call(
        kernel,
        out_shape=out_shape,
        in_specs=specs,
        out_specs=jax.tree.map(lambda _: outside if out_hbm else whole, out_shape),
        scratch_shapes=list(scratch),
        input_output_aliases=aliases or {},
        compiler_params=pltpu.CompilerParams(vmem_limit_bytes=limit),
        cost_estimate=pl.CostEstimate(
            flops=flops, bytes_accessed=sum(x.size * x.dtype.itemsize for x in inputs), transcendentals=0
        ),
        name=name,
    )(*inputs)


def shards(vis, coherency, gains_init, station_pairs):
    channels_dev = vis.shape[1]
    rows_dev = vis.shape[2]
    owned = gains_init.shape[3]
    pairs = lax.axis_size("pair")
    bands = lax.axis_size("freq")
    assert channels_dev == 2 * pairs and owned == 16 and STATION_TOTAL == 2 * owned * pairs
    assert ROUNDS == 2 and ITERS == 2
    weight = 2.0 * rows_dev * pairs * 2 / STATION_TOTAL
    swap = [(0, 1), (1, 0)]
    core = lax.axis_index("core").astype(i32).reshape(1)
    basis = lax.dynamic_slice_in_dim(
        jnp.asarray(basis_rows(channels_dev * bands)),
        lax.axis_index("freq") * channels_dev,
        channels_dev,
        1,
    )
    basis = basis.reshape(4, pairs, 1, 2, 1)
    basis = jnp.broadcast_to(basis, (4, pairs, SKY_DIRECTIONS, 2, LANES)).reshape(4, pairs, 8, LANES)
    shape = jax.ShapeDtypeStruct
    gains_shape = shape((2, 8, STATION_TOTAL), f32)
    sums_shape = shape((3, 8, STATION_TOTAL), f32)
    block_shape = shape((pairs, 8, LANES), f32)
    parts_shape = shape((bands, 8, LANES), f32)
    out_shape = shape((2, SKY_DIRECTIONS, owned, channels_dev), f32)
    width = 3 * rows_dev + LANES
    flops = 2 * rows_dev * pairs * 192 * 256
    scratch = [pltpu.VMEM((2 * LANES, 48 * PARTS), f32)]
    sweep = functools.partial(call, flops=flops, scratch=scratch)
    half_sweep = functools.partial(call, flops=flops // 2, scratch=scratch)

    def exchange(partial):
        return lax.ppermute(partial, "core", swap)

    def to_pairs(block):
        return lax.all_to_all(block, "pair", 0, 0, tiled=True)

    def over_bands(block):
        return lax.all_to_all(block, "freq", 0, 0, tiled=True)

    start = gains_init.transpose(0, 1, 3, 2)
    packed_shape = shape((pairs, 8, width), i16)
    packed = call(
        "pack",
        pack_kernel,
        packed_shape,
        coherency,
        vis,
        station_pairs,
        in_hbm=(0, 1, 2),
        out_hbm=True,
        limit=PACK_VMEM_LIMIT,
        scratch=[
            pltpu.VMEM(coherency.shape, bf16),
            pltpu.VMEM(vis.shape, f32),
            pltpu.VMEM(station_pairs.shape, i32),
            pltpu.VMEM(packed_shape.shape, i16),
            pltpu.SemaphoreType.DMA((2 * COPIES,)),
            pltpu.SemaphoreType.DMA((2 * COPIES,)),
            pltpu.SemaphoreType.DMA,
            pltpu.SemaphoreType.DMA((6 * COPIES,)),
        ],
    )
    packed = call(
        "seed",
        seed_kernel,
        packed_shape,
        core,
        start,
        exchange(start),
        packed,
        scalars=1,
        in_hbm=(3,),
        out_hbm=True,
        aliases={3: 0},
        limit=SEED_VMEM_LIMIT,
        scratch=[pltpu.VMEM((pairs, 8, LANES), i16), pltpu.SemaphoreType.DMA],
    )
    data = to_pairs(packed)

    sums, gains = sweep("first", first_kernel, (sums_shape, gains_shape), data)
    target = gains
    sums, gains = sweep(
        "step",
        functools.partial(step_kernel, weight),
        (sums_shape, gains_shape),
        data,
        sums,
        exchange(sums),
        gains,
    )
    finish = functools.partial(finish_kernel, weight)
    gains, block = call("finish", finish, (gains_shape, block_shape), sums, exchange(sums), gains, target)
    owner_gains = to_pairs(block)
    sums = half_sweep("early", early_kernel, sums_shape, data, gains)
    owner_gains, sums = lax.optimization_barrier((owner_gains, sums))
    parts = over_bands(call("fit", fit_kernel, parts_shape, basis, owner_gains))
    sums = half_sweep("late", late_kernel, sums_shape, data, gains, sums)
    parts, sums = lax.optimization_barrier((parts, sums))
    block, owner_dual = call(
        "spread", spread_kernel, (block_shape, block_shape), basis, parts, owner_gains
    )
    fit = to_pairs(block)

    sums, gains, target = sweep(
        "retarget",
        functools.partial(retarget_kernel, weight),
        (sums_shape, gains_shape, gains_shape),
        data,
        sums,
        exchange(sums),
        gains,
        fit,
    )
    gains, block = call("finish", finish, (gains_shape, block_shape), sums, exchange(sums), gains, target)
    owner_gains = to_pairs(block)
    parts = over_bands(call("fit", fit_kernel, parts_shape, basis, owner_gains, owner_dual))
    final_gains = call("place", place_kernel, out_shape, core, owner_gains, scalars=1)
    final_consensus = call("final", final_kernel, out_shape, core, basis, parts, scalars=1)
    return (final_gains.transpose(0, 1, 3, 2), final_consensus.transpose(0, 1, 3, 2))


def solution(mesh):
    split = Mesh(
        mesh.devices.reshape(mesh.shape["freq"], mesh.shape["bl"] // 2, 2), ("freq", "pair", "core")
    )
    bl = ("pair", "core")
    placed = (
        P(None, "freq", bl),
        P(None, None, "freq", bl),
        P(None, None, "freq", bl),
        P(None, bl),
    )
    return jax.shard_map(
        shards,
        mesh=split,
        in_specs=placed,
        out_specs=(P(None, None, "freq", bl), P(None, None, "freq", bl)),
        check_vma=False,
    )
```

```python
import functools

import jax
import jax.numpy as jnp
import numpy as np
from jax import lax
from jax.experimental import pallas as pl
from jax.experimental.pallas import tpu as pltpu
from jax.sharding import Mesh, PartitionSpec as P

STATION_TOTAL = 512
SKY_DIRECTIONS = 4
ITERS = 2
ROUNDS = 2
LANES = 128
PARTS = STATION_TOTAL // LANES
UNROLL = 8
COH_STEPS = 4096.0
GAIN_STEPS = 4096.0
REST_STEPS = 2.0**27
COPIES = 4
VMEM_LIMIT = 24 * 1024 * 1024
f32, bf16, i32, i16 = jnp.float32, jnp.bfloat16, jnp.int32, jnp.int16


def basis_rows(channels):
    position = (2.0 * np.arange(channels) + 1.0) / channels - 1.0
    rows = []
    for vector in [np.ones_like(position), position, position**2, position**3]:
        for other in rows:
            vector = vector - np.sum(other * vector) * other
        rows.append(vector / np.sqrt(np.sum(vector * vector)))
    return np.stack(rows).astype(np.float32)


def lanes_of(rows):
    return {"re": 0, "im": rows, "misc": 2 * rows, "start": 3 * rows}


def rows_of(data_ref):
    return (data_ref.shape[2] - LANES) // 3


def coded(values):
    return jnp.round(values).astype(i32).astype(i16)


def pick_channel_pair(by_direction, pair):
    return jnp.concatenate([block[2 * pair : 2 * pair + 2] for block in by_direction], 0)


def pack_kernel(
    coh_hbm, vis_hbm, pairs_hbm, out_ref, coh_ref, vis_ref, pairs_ref, coh_sem, vis_sem, pairs_sem
):
    rows = vis_ref.shape[2]
    count = out_ref.shape[0]
    channels = vis_ref.shape[1]
    at = lanes_of(rows)
    half = rows // 2
    piece = half // COPIES
    pairs_copy = pltpu.make_async_copy(pairs_hbm, pairs_ref, pairs_sem)
    pairs_copy.start()
    copies = []
    for index in range(COPIES):
        group = []
        for side in range(2):
            lanes = pl.ds(side * half + index * piece, piece)
            slot = 2 * index + side
            group.append(
                pltpu.make_async_copy(
                    coh_hbm.at[:, :, :, lanes], coh_ref.at[:, :, :, lanes], coh_sem.at[slot]
                )
            )
            group.append(
                pltpu.make_async_copy(vis_hbm.at[:, :, lanes], vis_ref.at[:, :, lanes], vis_sem.at[slot])
            )
        copies.append(group)
    for kind in (1, 0):
        for group in copies:
            for copy in group[kind::2]:
                copy.start()
    for group in copies:
        for copy in group[1::2]:
            copy.wait()
    peak = jnp.zeros((channels, LANES), f32)
    for start in range(0, rows, LANES):
        for part in range(2):
            peak = jnp.maximum(peak, jnp.abs(vis_ref[part, :, start : start + LANES]))
    peak = jnp.max(peak, axis=(0, 1), keepdims=True)
    exponent = jnp.full((1, 1), -60.0, f32)
    inverse = jnp.full((1, 1), 2.0**60, f32)
    for power in range(-60, -8):
        over = peak > 32767.0 * 2.0**power
        exponent = jnp.where(over, power + 1.0, exponent)
        inverse = jnp.where(over, 2.0 ** (-power - 1), inverse)
    exponent = jnp.broadcast_to(exponent, (2, LANES))

    def columns(index, carry):
        early = pl.multiple_of(index * LANES, LANES)
        late = pl.multiple_of(half + index * LANES, LANES)
        for offset in (early, late):
            lanes = pl.ds(offset, LANES)
            for part in range(2):
                blocks = [coh_ref[part, d, :, lanes].astype(f32) * COH_STEPS for d in range(SKY_DIRECTIONS)]
                place = pl.multiple_of(offset + part * rows, LANES)
                for p in range(count):
                    out_ref[p, :, pl.ds(place, LANES)] = coded(pick_channel_pair(blocks, p))
            seen = [vis_ref[part, :, lanes] * inverse for part in range(2)]
            tail = jnp.concatenate([pairs_ref[:, lanes].astype(f32), exponent], 0)
            place = pl.multiple_of(offset + at["misc"], LANES)
            for p in range(count):
                block = jnp.concatenate([seen[0][2 * p : 2 * p + 2], seen[1][2 * p : 2 * p + 2], tail], 0)
                out_ref[p, :, pl.ds(place, LANES)] = coded(block)
        return carry

    pairs_copy.wait()
    step = piece // LANES
    for index, group in enumerate(copies):
        for copy in group[0::2]:
            copy.wait()
        lax.fori_loop(index * step, (index + 1) * step, columns, 0)


def seed_kernel(core_ref, mine_ref, other_ref, packed_ref, out_ref, block_ref, block_sem):
    count = block_ref.shape[0]
    is_first = core_ref[0] == 0
    parts = []
    for part in range(2):
        mine = jnp.concatenate([mine_ref[part, d] for d in range(SKY_DIRECTIONS)], 1)
        other = jnp.concatenate([other_ref[part, d] for d in range(SKY_DIRECTIONS)], 1)
        start = jnp.concatenate([jnp.where(is_first, mine, other), jnp.where(is_first, other, mine)], 0)
        coarse = jnp.round(start * GAIN_STEPS)
        parts += [coarse, jnp.round((start - coarse * (1.0 / GAIN_STEPS)) * REST_STEPS)]
    square = jnp.concatenate(parts, 0).T
    blocks = [square[d * 2 * count : (d + 1) * 2 * count] for d in range(SKY_DIRECTIONS)]
    for p in range(count):
        block_ref[p] = coded(pick_channel_pair(blocks, p))
    width = out_ref.shape[2]
    copy = pltpu.make_async_copy(block_ref, out_ref.at[:, :, width - LANES : width], block_sem)
    copy.start()
    copy.wait()


def stations_in_lanes(pieces):
    lane = lax.broadcasted_iota(i32, (8, LANES), 1)
    tiles = []
    for q in range(0, len(pieces), 4):
        tile = pieces[q]
        for k in range(1, 4):
            moved = pltpu.roll(pieces[q + k], 32 * k, 1)
            tile = jnp.where(lane >= 32 * k, moved, tile)
        tiles.append(tile)
    return jnp.concatenate(tiles, 1)


def starting_gains(data_ref):
    at = lanes_of(rows_of(data_ref))["start"]
    parts = []
    for part in range(2):
        pieces = []
        for p in range(data_ref.shape[0]):
            piece = data_ref[p, :, at : at + LANES].astype(i32).astype(f32)
            if part:
                piece = pltpu.roll(piece, LANES - 64, 1)
            piece = piece * (1.0 / GAIN_STEPS) + pltpu.roll(piece, LANES - 32, 1) * (1.0 / REST_STEPS)
            pieces.append(piece)
        parts.append(stations_in_lanes(pieces))
    return parts


def lookup(words, low, high):
    picked = [jnp.take_along_axis(w, low, axis=1, mode="promise_in_bounds") for w in words]
    odd, upper = (high & 1) == 1, (high & 2) == 2
    word = jnp.where(
        upper, jnp.where(odd, picked[3], picked[2]), jnp.where(odd, picked[1], picked[0])
    )
    return (word >> 16).astype(f32), ((word & 65535) - 32768).astype(f32)


def words_of(gains_re, gains_im):
    rounded_re = gains_re.astype(bf16).astype(f32)
    rounded_im = gains_im.astype(bf16).astype(f32)
    peak = jnp.max(jnp.maximum(jnp.abs(rounded_re), jnp.abs(rounded_im)), axis=(0, 1), keepdims=True)
    unit = jnp.full((1, 1), 2.0**-60, f32)
    for power in range(-60, 60):
        unit = jnp.where(peak > 32767.0 * 2.0**power, 2.0 ** (power + 1), unit)
    inverse = 1.0 / unit
    scaled_re = jnp.round(rounded_re * inverse).astype(i32)
    scaled_im = jnp.round(rounded_im * inverse).astype(i32)
    word = (scaled_re << 16) + (scaled_im + 32768)
    return [word[:, h * LANES : (h + 1) * LANES] for h in range(PARTS)], unit


def column_terms(coh_re, coh_im, misc, vis_unit, words, square, sublane):
    def station(row):
        index = jnp.broadcast_to(misc[row : row + 1], (8, LANES))
        return index & (LANES - 1), index >> 7

    low_first, high_first = station(4)
    low_second, high_second = station(5)
    near_re, near_im = lookup(words, low_first, high_first)
    far_re, far_im = lookup(words, low_second, high_second)
    z_re = coh_re * far_re + coh_im * far_im
    z_im = coh_im * far_re - coh_re * far_im
    x_re = near_re * coh_re - near_im * coh_im
    x_im = near_re * coh_im + near_im * coh_re
    seen = misc.astype(f32) * vis_unit
    vis_re = jnp.where(sublane < 2, seen, 0.0)
    vis_im = jnp.where((sublane >= 2) & (sublane < 4), seen, 0.0)
    res_re = vis_re - square * (near_re * z_re - near_im * z_im)
    res_im = vis_im - square * (near_re * z_im + near_im * z_re)
    res_re = res_re + pltpu.roll(res_re, 4, 0)
    res_re = res_re + pltpu.roll(res_re, 2, 0)
    res_im = res_im + pltpu.roll(res_im, 4, 0)
    res_im = res_im + pltpu.roll(res_im, 2, 0)
    first = jnp.concatenate([res_re * z_re + res_im * z_im, res_im * z_re - res_re * z_im], 0)
    second = jnp.concatenate([res_re * x_re + res_im * x_im, res_re * x_im - res_im * x_re], 0)
    first_norm = z_re * z_re + z_im * z_im
    second_norm = x_re * x_re + x_im * x_im
    twice = lambda a: jnp.concatenate([a, a], 0).astype(bf16)
    return (
        (first.astype(bf16), twice(first_norm), low_first, high_first),
        (second.astype(bf16), twice(second_norm), low_second, high_second),
    )


def operands(term, station_rows, half_rows):
    pair, norm, low, high = term
    zero = jnp.zeros_like(pair)
    high = jnp.broadcast_to(high[:1], (16, LANES)).astype(i16)
    rows = [jnp.where(high == i16(h), pair, zero) for h in range(PARTS)]
    rows += [jnp.where(high == half_rows + i16(h), norm, zero) for h in range(0, PARTS, 2)]
    low = jnp.broadcast_to(low[:1].astype(f32), (LANES, LANES)).astype(bf16)
    table = jnp.where(station_rows == low, jnp.ones_like(low), jnp.zeros_like(low))
    return jnp.concatenate(rows, 0), table


def accumulate(data_ref, first, count, gains_re, gains_im, sums_ref, acc_ref, before=None):
    rows = rows_of(data_ref)
    at = lanes_of(rows)
    words, unit = words_of(gains_re, gains_im)
    square = jnp.broadcast_to(unit * unit * (1.0 / COH_STEPS), (8, LANES))
    unit = unit * (1.0 / COH_STEPS)
    station_rows = lax.broadcasted_iota(i32, (LANES, LANES), 0).astype(f32).astype(bf16)
    half_rows = (lax.broadcasted_iota(i32, (16, LANES), 0) >> 3).astype(i16)
    sublane = lax.broadcasted_iota(i32, (8, LANES), 0)
    acc_ref[...] = jnp.zeros_like(acc_ref)

    def step(source, carry):
        left, right = [], []
        exponent = data_ref[source, :, at["misc"] : at["misc"] + LANES].astype(i32).astype(f32)
        vis_unit = jnp.exp2(jnp.broadcast_to(exponent[6:7], (8, LANES)))
        for offset in range(0, rows, LANES):
            load = lambda start: data_ref[source, :, start : start + LANES].astype(i32)
            terms = column_terms(
                load(at["re"] + offset).astype(f32),
                load(at["im"] + offset).astype(f32),
                load(at["misc"] + offset),
                vis_unit,
                words,
                square,
                sublane,
            )
            (rows_first, table_first), (rows_second, table_second) = [
                operands(term, station_rows, half_rows) for term in terms
            ]
            left.append(jnp.concatenate([rows_first, rows_second], 0))
            right.append(jnp.concatenate([table_first, table_second], 0))
        acc_ref[...] += lax.dot_general(
            jnp.concatenate(right, 1),
            jnp.concatenate(left, 1),
            (((1,), (1,)), ((), ())),
            preferred_element_type=f32,
        )
        return carry

    lax.fori_loop(first, first + count, step, 0, unroll=UNROLL)
    tall = 24 * PARTS
    acc = (acc_ref[0:LANES, 0:tall] + acc_ref[LANES : 2 * LANES, tall : 2 * tall]).T
    base = 16 * PARTS
    sums = [
        jnp.concatenate([acc[16 * h : 16 * h + 8] for h in range(PARTS)], 1),
        jnp.concatenate([acc[16 * h + 8 : 16 * h + 16] for h in range(PARTS)], 1),
        jnp.concatenate([acc[base + 8 * h : base + 8 * h + 8] for h in range(PARTS)], 1),
    ]
    for k, factor in enumerate((unit, unit, unit * unit)):
        part = sums[k] * factor
        sums_ref[k] = part if before is None else before[k] + part


def advance(gains, sums, target, penalty_weight):
    return gains + (sums[0:2] + penalty_weight * (target - gains)) / (
        2.0 * sums[2] + penalty_weight
    )


def first_kernel(data_ref, sums_ref, gains_ref, acc_ref):
    gains = starting_gains(data_ref)
    gains_ref[0], gains_ref[1] = gains
    accumulate(data_ref, 0, data_ref.shape[0], *gains, sums_ref, acc_ref)


def early_kernel(data_ref, gains_ref, sums_ref, acc_ref):
    accumulate(data_ref, 0, data_ref.shape[0] // 2, gains_ref[0], gains_ref[1], sums_ref, acc_ref)


def late_kernel(data_ref, gains_ref, before_ref, sums_ref, acc_ref):
    half = data_ref.shape[0] // 2
    accumulate(data_ref, half, half, gains_ref[0], gains_ref[1], sums_ref, acc_ref, before_ref)


def step_kernel(weight, data_ref, mine_ref, other_ref, gains_ref, sums_ref, new_ref, acc_ref):
    gains = gains_ref[...]
    gains = advance(gains, mine_ref[...] + other_ref[...], gains, weight)
    new_ref[...] = gains
    accumulate(data_ref, 0, data_ref.shape[0], gains[0], gains[1], sums_ref, acc_ref)


def retarget_kernel(
    weight, data_ref, mine_ref, other_ref, gains_ref, fit_ref, sums_ref, new_ref, target_ref, acc_ref
):
    consensus = by_channel(fit_ref)
    gains = gains_ref[...]
    target = consensus - (gains - consensus)
    target_ref[...] = target
    gains = advance(gains, mine_ref[...] + other_ref[...], target, weight)
    new_ref[...] = gains
    accumulate(data_ref, 0, data_ref.shape[0], gains[0], gains[1], sums_ref, acc_ref)


def by_channel(block_ref):
    pieces = [block_ref[p] for p in range(block_ref.shape[0])]
    turned = [pltpu.roll(piece, LANES - 32, 1) for piece in pieces]
    return jnp.stack([stations_in_lanes(pieces), stations_in_lanes(turned)])


def finish_kernel(weight, mine_ref, other_ref, gains_ref, target_ref, new_ref, block_ref):
    gains = advance(gains_ref[...], mine_ref[...] + other_ref[...], target_ref[...], weight)
    new_ref[...] = gains
    lane = lax.broadcasted_iota(i32, (8, LANES), 1)
    for p in range(block_ref.shape[0]):
        tile = slice(p // 4 * LANES, (p // 4 + 1) * LANES)
        shift = 32 * (p % 4)
        real = pltpu.roll(gains[0][:, tile], (LANES - shift) % LANES, 1)
        imag = pltpu.roll(gains[1][:, tile], (LANES + 32 - shift) % LANES, 1)
        block_ref[p] = jnp.where(lane < 32, real, imag)


def is_even(shape):
    return (lax.broadcasted_iota(i32, shape, 0) & 1) == 0


def basis_column(basis_ref, row, source):
    return basis_ref[row, source]


def fit_kernel(basis_ref, *refs):
    *block_refs, out_ref = refs
    even = is_even((8, LANES))
    blocks = []
    for p in range(block_refs[0].shape[0]):
        blend = block_refs[0][p]
        if len(block_refs) > 1:
            blend = blend + block_refs[1][p]
        blocks.append(blend)
    totals = []
    for row in range(4):
        total = sum(basis_column(basis_ref, row, p) * block for p, block in enumerate(blocks))
        totals.append(total + jnp.where(even, pltpu.roll(total, 7, 0), pltpu.roll(total, 1, 0)))
    lane = lax.broadcasted_iota(i32, (8, LANES), 1)
    early = jnp.where(even, totals[0], totals[1])
    late = jnp.where(even, totals[2], totals[3])
    packed = jnp.where(lane < LANES // 2, early, pltpu.roll(late, LANES // 2, 1))
    for f in range(out_ref.shape[0]):
        out_ref[f] = packed


def consensus_blocks(basis_ref, parts_ref, count):
    even = is_even((8, LANES))
    total = parts_ref[0]
    for f in range(1, parts_ref.shape[0]):
        total = total + parts_ref[f]
    rows = []
    for half in (total, pltpu.roll(total, LANES // 2, 1)):
        rows.append(jnp.where(even, half, pltpu.roll(half, 1, 0)))
        rows.append(jnp.where(even, pltpu.roll(half, 7, 0), half))
    return [
        sum(basis_column(basis_ref, row, p) * rows[row] for row in range(4)) for p in range(count)
    ]


def spread_kernel(basis_ref, parts_ref, gains_ref, out_ref, dual_ref):
    for p, block in enumerate(consensus_blocks(basis_ref, parts_ref, out_ref.shape[0])):
        out_ref[p] = block
        dual_ref[p] = gains_ref[p] - block


def write_owned(blocks, is_first, out_ref):
    owned = out_ref.shape[2]
    channels = 2 * len(blocks)
    rows = [block[2 * d : 2 * d + 2] for d in range(SKY_DIRECTIONS) for block in blocks]
    turned = jnp.concatenate(rows, 0).T
    for part in range(2):
        both = turned[part * 2 * owned : (part + 1) * 2 * owned]
        mine = jnp.where(is_first, both[:owned], both[owned:])
        for d in range(SKY_DIRECTIONS):
            out_ref[part, d] = mine[:, d * channels : (d + 1) * channels]


def place_kernel(core_ref, blocks_ref, out_ref):
    write_owned([blocks_ref[p] for p in range(blocks_ref.shape[0])], core_ref[0] == 0, out_ref)


def final_kernel(core_ref, basis_ref, parts_ref, out_ref):
    count = out_ref.shape[3] // 2
    write_owned(consensus_blocks(basis_ref, parts_ref, count), core_ref[0] == 0, out_ref)


def call(
    name,
    kernel,
    out_shape,
    *inputs,
    scalars=0,
    outside=(),
    aliases=None,
    flops=0,
    scratch=(),
):
    whole = pl.BlockSpec(memory_space=pltpu.VMEM)
    anywhere = pl.BlockSpec(memory_space=pl.ANY)
    specs = [pl.BlockSpec(memory_space=pltpu.SMEM)] * scalars
    specs += [anywhere if k in outside else whole for k in range(scalars, len(inputs))]
    return pl.pallas_call(
        kernel,
        out_shape=out_shape,
        in_specs=specs,
        out_specs=jax.tree.map(lambda _: anywhere if aliases else whole, out_shape),
        scratch_shapes=list(scratch),
        input_output_aliases=aliases or {},
        compiler_params=pltpu.CompilerParams(vmem_limit_bytes=VMEM_LIMIT),
        cost_estimate=pl.CostEstimate(
            flops=flops, bytes_accessed=sum(x.size * x.dtype.itemsize for x in inputs), transcendentals=0
        ),
        name=name,
    )(*inputs)


def shards(vis, coherency, gains_init, station_pairs):
    channels_dev = vis.shape[1]
    rows_dev = vis.shape[2]
    owned = gains_init.shape[3]
    pairs = lax.axis_size("pair")
    bands = lax.axis_size("freq")
    assert channels_dev == 2 * pairs and owned == 16 and STATION_TOTAL == 2 * owned * pairs
    assert ROUNDS == 2 and ITERS == 2
    weight = 2.0 * rows_dev * pairs * 2 / STATION_TOTAL
    swap = [(0, 1), (1, 0)]
    core = lax.axis_index("core").astype(i32).reshape(1)
    basis = lax.dynamic_slice_in_dim(
        jnp.asarray(basis_rows(channels_dev * bands)),
        lax.axis_index("freq") * channels_dev,
        channels_dev,
        1,
    )
    basis = basis.reshape(4, pairs, 1, 2, 1)
    basis = jnp.broadcast_to(basis, (4, pairs, SKY_DIRECTIONS, 2, LANES)).reshape(4, pairs, 8, LANES)
    shape = jax.ShapeDtypeStruct
    gains_shape = shape((2, 8, STATION_TOTAL), f32)
    sums_shape = shape((3, 8, STATION_TOTAL), f32)
    block_shape = shape((pairs, 8, LANES), f32)
    parts_shape = shape((bands, 8, LANES), f32)
    out_shape = shape((2, SKY_DIRECTIONS, owned, channels_dev), f32)
    width = 3 * rows_dev + LANES
    flops = 2 * rows_dev * pairs * 192 * 256
    scratch = [pltpu.VMEM((2 * LANES, 48 * PARTS), f32)]
    sweep = functools.partial(call, flops=flops, scratch=scratch)
    half_sweep = functools.partial(call, flops=flops // 2, scratch=scratch)

    def in_hbm(array):
        return pltpu.with_memory_space_constraint(array, pltpu.HBM)

    def exchange(partial):
        return lax.ppermute(partial, "core", swap)

    def to_pairs(block):
        return lax.all_to_all(block, "pair", 0, 0, tiled=True)

    def over_bands(block):
        return lax.all_to_all(block, "freq", 0, 0, tiled=True)

    start = gains_init.transpose(0, 1, 3, 2)
    packed_shape = shape((pairs, 8, width), i16)
    packed = call(
        "pack",
        pack_kernel,
        packed_shape,
        in_hbm(coherency),
        in_hbm(vis),
        in_hbm(station_pairs),
        outside=(0, 1, 2),
        scratch=[
            pltpu.VMEM(coherency.shape, bf16),
            pltpu.VMEM(vis.shape, f32),
            pltpu.VMEM(station_pairs.shape, i32),
            pltpu.SemaphoreType.DMA((2 * COPIES,)),
            pltpu.SemaphoreType.DMA((2 * COPIES,)),
            pltpu.SemaphoreType.DMA,
        ],
    )
    packed = call(
        "seed",
        seed_kernel,
        packed_shape,
        core,
        start,
        exchange(start),
        packed,
        scalars=1,
        outside=(3,),
        aliases={3: 0},
        scratch=[pltpu.VMEM((pairs, 8, LANES), i16), pltpu.SemaphoreType.DMA],
    )
    data = to_pairs(packed)

    sums, gains = sweep("first", first_kernel, (sums_shape, gains_shape), data)
    target = gains
    sums, gains = sweep(
        "step",
        functools.partial(step_kernel, weight),
        (sums_shape, gains_shape),
        data,
        sums,
        exchange(sums),
        gains,
    )
    finish = functools.partial(finish_kernel, weight)
    gains, block = call("finish", finish, (gains_shape, block_shape), sums, exchange(sums), gains, target)
    owner_gains = to_pairs(block)
    sums = half_sweep("early", early_kernel, sums_shape, data, gains)
    owner_gains, sums = lax.optimization_barrier((owner_gains, sums))
    parts = over_bands(call("fit", fit_kernel, parts_shape, basis, owner_gains))
    sums = half_sweep("late", late_kernel, sums_shape, data, gains, sums)
    parts, sums = lax.optimization_barrier((parts, sums))
    block, owner_dual = call(
        "spread", spread_kernel, (block_shape, block_shape), basis, parts, owner_gains
    )
    fit = to_pairs(block)

    sums, gains, target = sweep(
        "retarget",
        functools.partial(retarget_kernel, weight),
        (sums_shape, gains_shape, gains_shape),
        data,
        sums,
        exchange(sums),
        gains,
        fit,
    )
    gains, block = call("finish", finish, (gains_shape, block_shape), sums, exchange(sums), gains, target)
    owner_gains = to_pairs(block)
    parts = over_bands(call("fit", fit_kernel, parts_shape, basis, owner_gains, owner_dual))
    final_gains = call("place", place_kernel, out_shape, core, owner_gains, scalars=1)
    final_consensus = call("final", final_kernel, out_shape, core, basis, parts, scalars=1)
    return (final_gains.transpose(0, 1, 3, 2), final_consensus.transpose(0, 1, 3, 2))


def solution(mesh):
    split = Mesh(
        mesh.devices.reshape(mesh.shape["freq"], mesh.shape["bl"] // 2, 2), ("freq", "pair", "core")
    )
    bl = ("pair", "core")
    placed = (
        P(None, "freq", bl),
        P(None, None, "freq", bl),
        P(None, None, "freq", bl),
        P(None, bl),
    )
    return jax.shard_map(
        shards,
        mesh=split,
        in_specs=placed,
        out_specs=(P(None, None, "freq", bl), P(None, None, "freq", bl)),
        check_vma=False,
    )
```

```python
import functools

import jax
import jax.numpy as jnp
import numpy as np
from jax import lax
from jax.experimental import pallas as pl
from jax.experimental.pallas import tpu as pltpu
from jax.sharding import Mesh, PartitionSpec as P

STATION_TOTAL = 512
SKY_DIRECTIONS = 4
ITERS = 2
ROUNDS = 2
LANES = 128
PARTS = STATION_TOTAL // LANES
UNROLL = 8
COH_STEPS = 4096.0
GAIN_STEPS = 4096.0
REST_STEPS = 2.0**27
COPIES = 4
VMEM_LIMIT = 24 * 1024 * 1024
f32, bf16, i32, i16 = jnp.float32, jnp.bfloat16, jnp.int32, jnp.int16


def basis_rows(channels):
    position = (2.0 * np.arange(channels) + 1.0) / channels - 1.0
    rows = []
    for vector in [np.ones_like(position), position, position**2, position**3]:
        for other in rows:
            vector = vector - np.sum(other * vector) * other
        rows.append(vector / np.sqrt(np.sum(vector * vector)))
    return np.stack(rows).astype(np.float32)


def lanes_of(rows):
    start = 2 * rows + 3 * rows // 4
    return {"re": 0, "im": rows, "misc": 2 * rows, "start": start, "scale": start + LANES}


def rows_of(data_ref):
    return (data_ref.shape[2] - 2 * LANES) * 4 // 11


def coded(values):
    return jnp.round(values).astype(i32).astype(i16)


def pick_channel_pair(by_direction, pair):
    return jnp.concatenate([block[2 * pair : 2 * pair + 2] for block in by_direction], 0)


def pack_kernel(
    coh_hbm, vis_hbm, pairs_hbm, out_ref, coh_ref, vis_ref, pairs_ref, coh_sem, vis_sem, pairs_sem
):
    rows = vis_ref.shape[2]
    count = out_ref.shape[0]
    channels = vis_ref.shape[1]
    at = lanes_of(rows)
    half = rows // 2
    piece = half // COPIES
    pairs_copy = pltpu.make_async_copy(pairs_hbm, pairs_ref, pairs_sem)
    pairs_copy.start()
    copies = []
    for index in range(COPIES):
        group = []
        for side in range(2):
            lanes = pl.ds(side * half + index * piece, piece)
            slot = 2 * index + side
            group.append(
                pltpu.make_async_copy(
                    coh_hbm.at[:, :, :, lanes], coh_ref.at[:, :, :, lanes], coh_sem.at[slot]
                )
            )
            group.append(
                pltpu.make_async_copy(vis_hbm.at[:, :, lanes], vis_ref.at[:, :, lanes], vis_sem.at[slot])
            )
        copies.append(group)
    for kind in (1, 0):
        for group in copies:
            for copy in group[kind::2]:
                copy.start()
    for group in copies:
        for copy in group[1::2]:
            copy.wait()
    peak = jnp.zeros((channels, LANES), f32)
    for start in range(0, rows, LANES):
        for part in range(2):
            peak = jnp.maximum(peak, jnp.abs(vis_ref[part, :, start : start + LANES]))
    peak = jnp.max(peak, axis=(0, 1), keepdims=True)
    exponent = jnp.full((1, 1), -60.0, f32)
    inverse = jnp.full((1, 1), 2.0**60, f32)
    for power in range(-60, -8):
        over = peak > 32767.0 * 2.0**power
        exponent = jnp.where(over, power + 1.0, exponent)
        inverse = jnp.where(over, 2.0 ** (-power - 1), inverse)
    exponent = coded(jnp.broadcast_to(exponent, (8, LANES)))
    for p in range(count):
        out_ref[p, :, at["scale"] : at["scale"] + LANES] = exponent
    pairs_copy.wait()

    def misc(group, carry):
        columns = [pl.ds(pl.multiple_of((4 * group + k) * LANES, LANES), LANES) for k in range(4)]
        stations = coded(jnp.concatenate([pairs_ref[:, lanes].astype(f32) for lanes in columns], 0))
        seen = [[vis_ref[part, :, lanes] * inverse for lanes in columns] for part in range(2)]
        place = at["misc"] + 3 * LANES * group
        places = [pl.ds(pl.multiple_of(place + k * LANES, LANES), LANES) for k in range(3)]
        for p in range(count):
            out_ref[p, :, places[0]] = coded(pick_channel_pair(seen[0], p))
            out_ref[p, :, places[1]] = coded(pick_channel_pair(seen[1], p))
            out_ref[p, :, places[2]] = stations
        return carry

    lax.fori_loop(0, rows // (4 * LANES), misc, 0)

    def columns(index, carry):
        early = pl.multiple_of(index * LANES, LANES)
        late = pl.multiple_of(half + index * LANES, LANES)
        for offset in (early, late):
            lanes = pl.ds(offset, LANES)
            for part in range(2):
                blocks = [coh_ref[part, d, :, lanes].astype(f32) * COH_STEPS for d in range(SKY_DIRECTIONS)]
                place = pl.multiple_of(offset + part * rows, LANES)
                for p in range(count):
                    out_ref[p, :, pl.ds(place, LANES)] = coded(pick_channel_pair(blocks, p))
        return carry

    step = piece // LANES
    for index, group in enumerate(copies):
        for copy in group[0::2]:
            copy.wait()
        lax.fori_loop(index * step, (index + 1) * step, columns, 0)


def seed_kernel(core_ref, mine_ref, other_ref, packed_ref, out_ref, block_ref, block_sem):
    count = block_ref.shape[0]
    is_first = core_ref[0] == 0
    parts = []
    for part in range(2):
        mine = jnp.concatenate([mine_ref[part, d] for d in range(SKY_DIRECTIONS)], 1)
        other = jnp.concatenate([other_ref[part, d] for d in range(SKY_DIRECTIONS)], 1)
        start = jnp.concatenate([jnp.where(is_first, mine, other), jnp.where(is_first, other, mine)], 0)
        coarse = jnp.round(start * GAIN_STEPS)
        parts += [coarse, jnp.round((start - coarse * (1.0 / GAIN_STEPS)) * REST_STEPS)]
    square = jnp.concatenate(parts, 0).T
    blocks = [square[d * 2 * count : (d + 1) * 2 * count] for d in range(SKY_DIRECTIONS)]
    for p in range(count):
        block_ref[p] = coded(pick_channel_pair(blocks, p))
    width = out_ref.shape[2]
    copy = pltpu.make_async_copy(block_ref, out_ref.at[:, :, width - 2 * LANES : width - LANES], block_sem)
    copy.start()
    copy.wait()


def stations_in_lanes(pieces):
    lane = lax.broadcasted_iota(i32, (8, LANES), 1)
    tiles = []
    for q in range(0, len(pieces), 4):
        tile = pieces[q]
        for k in range(1, 4):
            moved = pltpu.roll(pieces[q + k], 32 * k, 1)
            tile = jnp.where(lane >= 32 * k, moved, tile)
        tiles.append(tile)
    return jnp.concatenate(tiles, 1)


def starting_gains(data_ref):
    at = lanes_of(rows_of(data_ref))["start"]
    parts = []
    for part in range(2):
        pieces = []
        for p in range(data_ref.shape[0]):
            piece = data_ref[p, :, at : at + LANES].astype(i32).astype(f32)
            if part:
                piece = pltpu.roll(piece, LANES - 64, 1)
            piece = piece * (1.0 / GAIN_STEPS) + pltpu.roll(piece, LANES - 32, 1) * (1.0 / REST_STEPS)
            pieces.append(piece)
        parts.append(stations_in_lanes(pieces))
    return parts


def lookup(words, low, high):
    picked = [jnp.take_along_axis(w, low, axis=1, mode="promise_in_bounds") for w in words]
    odd, upper = (high & 1) == 1, (high & 2) == 2
    word = jnp.where(
        upper, jnp.where(odd, picked[3], picked[2]), jnp.where(odd, picked[1], picked[0])
    )
    return (word >> 16).astype(f32), ((word & 65535) - 32768).astype(f32)


def words_of(gains_re, gains_im):
    rounded_re = gains_re.astype(bf16).astype(f32)
    rounded_im = gains_im.astype(bf16).astype(f32)
    peak = jnp.max(jnp.maximum(jnp.abs(rounded_re), jnp.abs(rounded_im)), axis=(0, 1), keepdims=True)
    unit = jnp.full((1, 1), 2.0**-60, f32)
    for power in range(-60, 60):
        unit = jnp.where(peak > 32767.0 * 2.0**power, 2.0 ** (power + 1), unit)
    inverse = 1.0 / unit
    scaled_re = jnp.round(rounded_re * inverse).astype(i32)
    scaled_im = jnp.round(rounded_im * inverse).astype(i32)
    word = (scaled_re << 16) + (scaled_im + 32768)
    return [word[:, h * LANES : (h + 1) * LANES] for h in range(PARTS)], unit


def column_terms(coh_re, coh_im, seen_re, seen_im, stations, place, words, square, sublane):
    def station(row):
        index = jnp.broadcast_to(stations[row : row + 1], (8, LANES))
        return index & (LANES - 1), index >> 7

    low_first, high_first = station(2 * place)
    low_second, high_second = station(2 * place + 1)
    near_re, near_im = lookup(words, low_first, high_first)
    far_re, far_im = lookup(words, low_second, high_second)
    z_re = coh_re * far_re + coh_im * far_im
    z_im = coh_im * far_re - coh_re * far_im
    x_re = near_re * coh_re - near_im * coh_im
    x_im = near_re * coh_im + near_im * coh_re
    inside = (sublane >> 1) == place
    vis_re = jnp.where(inside, seen_re, 0.0)
    vis_im = jnp.where(inside, seen_im, 0.0)
    res_re = vis_re - square * (near_re * z_re - near_im * z_im)
    res_im = vis_im - square * (near_re * z_im + near_im * z_re)
    res_re = res_re + pltpu.roll(res_re, 4, 0)
    res_re = res_re + pltpu.roll(res_re, 2, 0)
    res_im = res_im + pltpu.roll(res_im, 4, 0)
    res_im = res_im + pltpu.roll(res_im, 2, 0)
    first = jnp.concatenate([res_re * z_re + res_im * z_im, res_im * z_re - res_re * z_im], 0)
    second = jnp.concatenate([res_re * x_re + res_im * x_im, res_re * x_im - res_im * x_re], 0)
    first_norm = z_re * z_re + z_im * z_im
    second_norm = x_re * x_re + x_im * x_im
    twice = lambda a: jnp.concatenate([a, a], 0).astype(bf16)
    return (
        (first.astype(bf16), twice(first_norm), low_first, high_first),
        (second.astype(bf16), twice(second_norm), low_second, high_second),
    )


def operands(term, station_rows, half_rows):
    pair, norm, low, high = term
    zero = jnp.zeros_like(pair)
    high = jnp.broadcast_to(high[:1], (16, LANES)).astype(i16)
    rows = [jnp.where(high == i16(h), pair, zero) for h in range(PARTS)]
    rows += [jnp.where(high == half_rows + i16(h), norm, zero) for h in range(0, PARTS, 2)]
    low = jnp.broadcast_to(low[:1].astype(f32), (LANES, LANES)).astype(bf16)
    table = jnp.where(station_rows == low, jnp.ones_like(low), jnp.zeros_like(low))
    return jnp.concatenate(rows, 0), table


def accumulate(data_ref, first, count, gains_re, gains_im, sums_ref, acc_ref, before=None):
    rows = rows_of(data_ref)
    at = lanes_of(rows)
    words, unit = words_of(gains_re, gains_im)
    square = jnp.broadcast_to(unit * unit * (1.0 / COH_STEPS), (8, LANES))
    unit = unit * (1.0 / COH_STEPS)
    station_rows = lax.broadcasted_iota(i32, (LANES, LANES), 0).astype(f32).astype(bf16)
    half_rows = (lax.broadcasted_iota(i32, (16, LANES), 0) >> 3).astype(i16)
    sublane = lax.broadcasted_iota(i32, (8, LANES), 0)
    acc_ref[...] = jnp.zeros_like(acc_ref)

    def step(source, carry):
        left, right = [], []
        load = lambda start: data_ref[source, :, start : start + LANES].astype(i32)
        vis_unit = jnp.exp2(load(at["scale"]).astype(f32))
        for offset in range(0, rows, LANES):
            place = offset // LANES % 4
            if place == 0:
                group = at["misc"] + 3 * offset // 4
                seen_re = load(group).astype(f32) * vis_unit
                seen_im = load(group + LANES).astype(f32) * vis_unit
                stations = load(group + 2 * LANES)
            terms = column_terms(
                load(at["re"] + offset).astype(f32),
                load(at["im"] + offset).astype(f32),
                seen_re,
                seen_im,
                stations,
                place,
                words,
                square,
                sublane,
            )
            (rows_first, table_first), (rows_second, table_second) = [
                operands(term, station_rows, half_rows) for term in terms
            ]
            left.append(jnp.concatenate([rows_first, rows_second], 0))
            right.append(jnp.concatenate([table_first, table_second], 0))
        acc_ref[...] += lax.dot_general(
            jnp.concatenate(right, 1),
            jnp.concatenate(left, 1),
            (((1,), (1,)), ((), ())),
            preferred_element_type=f32,
        )
        return carry

    lax.fori_loop(first, first + count, step, 0, unroll=UNROLL)
    tall = 24 * PARTS
    acc = (acc_ref[0:LANES, 0:tall] + acc_ref[LANES : 2 * LANES, tall : 2 * tall]).T
    base = 16 * PARTS
    sums = [
        jnp.concatenate([acc[16 * h : 16 * h + 8] for h in range(PARTS)], 1),
        jnp.concatenate([acc[16 * h + 8 : 16 * h + 16] for h in range(PARTS)], 1),
        jnp.concatenate([acc[base + 8 * h : base + 8 * h + 8] for h in range(PARTS)], 1),
    ]
    for k, factor in enumerate((unit, unit, unit * unit)):
        part = sums[k] * factor
        sums_ref[k] = part if before is None else before[k] + part


def advance(gains, sums, target, penalty_weight):
    return gains + (sums[0:2] + penalty_weight * (target - gains)) / (
        2.0 * sums[2] + penalty_weight
    )


def first_kernel(data_ref, sums_ref, gains_ref, acc_ref):
    gains = starting_gains(data_ref)
    gains_ref[0], gains_ref[1] = gains
    accumulate(data_ref, 0, data_ref.shape[0], *gains, sums_ref, acc_ref)


def early_kernel(data_ref, gains_ref, sums_ref, acc_ref):
    accumulate(data_ref, 0, data_ref.shape[0] // 2, gains_ref[0], gains_ref[1], sums_ref, acc_ref)


def late_kernel(data_ref, gains_ref, before_ref, sums_ref, acc_ref):
    half = data_ref.shape[0] // 2
    accumulate(data_ref, half, half, gains_ref[0], gains_ref[1], sums_ref, acc_ref, before_ref)


def step_kernel(weight, data_ref, mine_ref, other_ref, gains_ref, sums_ref, new_ref, acc_ref):
    gains = gains_ref[...]
    gains = advance(gains, mine_ref[...] + other_ref[...], gains, weight)
    new_ref[...] = gains
    accumulate(data_ref, 0, data_ref.shape[0], gains[0], gains[1], sums_ref, acc_ref)


def retarget_kernel(
    weight, data_ref, mine_ref, other_ref, gains_ref, fit_ref, sums_ref, new_ref, target_ref, acc_ref
):
    consensus = by_channel(fit_ref)
    gains = gains_ref[...]
    target = consensus - (gains - consensus)
    target_ref[...] = target
    gains = advance(gains, mine_ref[...] + other_ref[...], target, weight)
    new_ref[...] = gains
    accumulate(data_ref, 0, data_ref.shape[0], gains[0], gains[1], sums_ref, acc_ref)


def by_channel(block_ref):
    pieces = [block_ref[p] for p in range(block_ref.shape[0])]
    turned = [pltpu.roll(piece, LANES - 32, 1) for piece in pieces]
    return jnp.stack([stations_in_lanes(pieces), stations_in_lanes(turned)])


def finish_kernel(weight, mine_ref, other_ref, gains_ref, target_ref, new_ref, block_ref):
    gains = advance(gains_ref[...], mine_ref[...] + other_ref[...], target_ref[...], weight)
    new_ref[...] = gains
    lane = lax.broadcasted_iota(i32, (8, LANES), 1)
    for p in range(block_ref.shape[0]):
        tile = slice(p // 4 * LANES, (p // 4 + 1) * LANES)
        shift = 32 * (p % 4)
        real = pltpu.roll(gains[0][:, tile], (LANES - shift) % LANES, 1)
        imag = pltpu.roll(gains[1][:, tile], (LANES + 32 - shift) % LANES, 1)
        block_ref[p] = jnp.where(lane < 32, real, imag)


def is_even(shape):
    return (lax.broadcasted_iota(i32, shape, 0) & 1) == 0


def basis_column(basis_ref, row, source):
    return basis_ref[row, source]


def fit_kernel(basis_ref, *refs):
    *block_refs, out_ref = refs
    even = is_even((8, LANES))
    blocks = []
    for p in range(block_refs[0].shape[0]):
        blend = block_refs[0][p]
        if len(block_refs) > 1:
            blend = blend + block_refs[1][p]
        blocks.append(blend)
    totals = []
    for row in range(4):
        total = sum(basis_column(basis_ref, row, p) * block for p, block in enumerate(blocks))
        totals.append(total + jnp.where(even, pltpu.roll(total, 7, 0), pltpu.roll(total, 1, 0)))
    lane = lax.broadcasted_iota(i32, (8, LANES), 1)
    early = jnp.where(even, totals[0], totals[1])
    late = jnp.where(even, totals[2], totals[3])
    packed = jnp.where(lane < LANES // 2, early, pltpu.roll(late, LANES // 2, 1))
    for f in range(out_ref.shape[0]):
        out_ref[f] = packed


def consensus_blocks(basis_ref, parts_ref, count):
    even = is_even((8, LANES))
    total = parts_ref[0]
    for f in range(1, parts_ref.shape[0]):
        total = total + parts_ref[f]
    rows = []
    for half in (total, pltpu.roll(total, LANES // 2, 1)):
        rows.append(jnp.where(even, half, pltpu.roll(half, 1, 0)))
        rows.append(jnp.where(even, pltpu.roll(half, 7, 0), half))
    return [
        sum(basis_column(basis_ref, row, p) * rows[row] for row in range(4)) for p in range(count)
    ]


def spread_kernel(basis_ref, parts_ref, gains_ref, out_ref, dual_ref):
    for p, block in enumerate(consensus_blocks(basis_ref, parts_ref, out_ref.shape[0])):
        out_ref[p] = block
        dual_ref[p] = gains_ref[p] - block


def write_owned(blocks, is_first, out_ref):
    owned = out_ref.shape[2]
    channels = 2 * len(blocks)
    rows = [block[2 * d : 2 * d + 2] for d in range(SKY_DIRECTIONS) for block in blocks]
    turned = jnp.concatenate(rows, 0).T
    for part in range(2):
        both = turned[part * 2 * owned : (part + 1) * 2 * owned]
        mine = jnp.where(is_first, both[:owned], both[owned:])
        for d in range(SKY_DIRECTIONS):
            out_ref[part, d] = mine[:, d * channels : (d + 1) * channels]


def place_kernel(core_ref, blocks_ref, out_ref):
    write_owned([blocks_ref[p] for p in range(blocks_ref.shape[0])], core_ref[0] == 0, out_ref)


def final_kernel(core_ref, basis_ref, parts_ref, out_ref):
    count = out_ref.shape[3] // 2
    write_owned(consensus_blocks(basis_ref, parts_ref, count), core_ref[0] == 0, out_ref)


def call(
    name,
    kernel,
    out_shape,
    *inputs,
    scalars=0,
    outside=(),
    aliases=None,
    flops=0,
    scratch=(),
):
    whole = pl.BlockSpec(memory_space=pltpu.VMEM)
    anywhere = pl.BlockSpec(memory_space=pl.ANY)
    specs = [pl.BlockSpec(memory_space=pltpu.SMEM)] * scalars
    specs += [anywhere if k in outside else whole for k in range(scalars, len(inputs))]
    return pl.pallas_call(
        kernel,
        out_shape=out_shape,
        in_specs=specs,
        out_specs=jax.tree.map(lambda _: anywhere if aliases else whole, out_shape),
        scratch_shapes=list(scratch),
        input_output_aliases=aliases or {},
        compiler_params=pltpu.CompilerParams(vmem_limit_bytes=VMEM_LIMIT),
        cost_estimate=pl.CostEstimate(
            flops=flops, bytes_accessed=sum(x.size * x.dtype.itemsize for x in inputs), transcendentals=0
        ),
        name=name,
    )(*inputs)


def shards(vis, coherency, gains_init, station_pairs):
    channels_dev = vis.shape[1]
    rows_dev = vis.shape[2]
    owned = gains_init.shape[3]
    pairs = lax.axis_size("pair")
    bands = lax.axis_size("freq")
    assert channels_dev == 2 * pairs and owned == 16 and STATION_TOTAL == 2 * owned * pairs
    assert ROUNDS == 2 and ITERS == 2
    weight = 2.0 * rows_dev * pairs * 2 / STATION_TOTAL
    swap = [(0, 1), (1, 0)]
    core = lax.axis_index("core").astype(i32).reshape(1)
    basis = lax.dynamic_slice_in_dim(
        jnp.asarray(basis_rows(channels_dev * bands)),
        lax.axis_index("freq") * channels_dev,
        channels_dev,
        1,
    )
    basis = basis.reshape(4, pairs, 1, 2, 1)
    basis = jnp.broadcast_to(basis, (4, pairs, SKY_DIRECTIONS, 2, LANES)).reshape(4, pairs, 8, LANES)
    shape = jax.ShapeDtypeStruct
    gains_shape = shape((2, 8, STATION_TOTAL), f32)
    sums_shape = shape((3, 8, STATION_TOTAL), f32)
    block_shape = shape((pairs, 8, LANES), f32)
    parts_shape = shape((bands, 8, LANES), f32)
    out_shape = shape((2, SKY_DIRECTIONS, owned, channels_dev), f32)
    width = 11 * rows_dev // 4 + 2 * LANES
    flops = 2 * rows_dev * pairs * 192 * 256
    scratch = [pltpu.VMEM((2 * LANES, 48 * PARTS), f32)]
    sweep = functools.partial(call, flops=flops, scratch=scratch)
    half_sweep = functools.partial(call, flops=flops // 2, scratch=scratch)

    def in_hbm(array):
        return pltpu.with_memory_space_constraint(array, pltpu.HBM)

    def exchange(partial):
        return lax.ppermute(partial, "core", swap)

    def to_pairs(block):
        return lax.all_to_all(block, "pair", 0, 0, tiled=True)

    def over_bands(block):
        return lax.all_to_all(block, "freq", 0, 0, tiled=True)

    start = gains_init.transpose(0, 1, 3, 2)
    packed_shape = shape((pairs, 8, width), i16)
    packed = call(
        "pack",
        pack_kernel,
        packed_shape,
        in_hbm(coherency),
        in_hbm(vis),
        in_hbm(station_pairs),
        outside=(0, 1, 2),
        scratch=[
            pltpu.VMEM(coherency.shape, bf16),
            pltpu.VMEM(vis.shape, f32),
            pltpu.VMEM(station_pairs.shape, i32),
            pltpu.SemaphoreType.DMA((2 * COPIES,)),
            pltpu.SemaphoreType.DMA((2 * COPIES,)),
            pltpu.SemaphoreType.DMA,
        ],
    )
    packed = call(
        "seed",
        seed_kernel,
        packed_shape,
        core,
        start,
        exchange(start),
        packed,
        scalars=1,
        outside=(3,),
        aliases={3: 0},
        scratch=[pltpu.VMEM((pairs, 8, LANES), i16), pltpu.SemaphoreType.DMA],
    )
    data = to_pairs(packed)

    sums, gains = sweep("first", first_kernel, (sums_shape, gains_shape), data)
    target = gains
    sums, gains = sweep(
        "step",
        functools.partial(step_kernel, weight),
        (sums_shape, gains_shape),
        data,
        sums,
        exchange(sums),
        gains,
    )
    finish = functools.partial(finish_kernel, weight)
    gains, block = call("finish", finish, (gains_shape, block_shape), sums, exchange(sums), gains, target)
    owner_gains = to_pairs(block)
    sums = half_sweep("early", early_kernel, sums_shape, data, gains)
    owner_gains, sums = lax.optimization_barrier((owner_gains, sums))
    parts = over_bands(call("fit", fit_kernel, parts_shape, basis, owner_gains))
    sums = half_sweep("late", late_kernel, sums_shape, data, gains, sums)
    parts, sums = lax.optimization_barrier((parts, sums))
    block, owner_dual = call(
        "spread", spread_kernel, (block_shape, block_shape), basis, parts, owner_gains
    )
    fit = to_pairs(block)

    sums, gains, target = sweep(
        "retarget",
        functools.partial(retarget_kernel, weight),
        (sums_shape, gains_shape, gains_shape),
        data,
        sums,
        exchange(sums),
        gains,
        fit,
    )
    gains, block = call("finish", finish, (gains_shape, block_shape), sums, exchange(sums), gains, target)
    owner_gains = to_pairs(block)
    parts = over_bands(call("fit", fit_kernel, parts_shape, basis, owner_gains, owner_dual))
    final_gains = call("place", place_kernel, out_shape, core, owner_gains, scalars=1)
    final_consensus = call("final", final_kernel, out_shape, core, basis, parts, scalars=1)
    return (final_gains.transpose(0, 1, 3, 2), final_consensus.transpose(0, 1, 3, 2))


def solution(mesh):
    split = Mesh(
        mesh.devices.reshape(mesh.shape["freq"], mesh.shape["bl"] // 2, 2), ("freq", "pair", "core")
    )
    bl = ("pair", "core")
    placed = (
        P(None, "freq", bl),
        P(None, None, "freq", bl),
        P(None, None, "freq", bl),
        P(None, bl),
    )
    return jax.shard_map(
        shards,
        mesh=split,
        in_specs=placed,
        out_specs=(P(None, None, "freq", bl), P(None, None, "freq", bl)),
        check_vma=False,
    )
```

```python
import functools

import jax
import jax.numpy as jnp
import numpy as np
from jax import lax
from jax.experimental import pallas as pl
from jax.experimental.pallas import tpu as pltpu
from jax.sharding import Mesh, PartitionSpec as P

STATION_TOTAL = 512
SKY_DIRECTIONS = 4
ITERS = 2
ROUNDS = 2
LANES = 128
PARTS = STATION_TOTAL // LANES
UNROLL = 8
COH_STEPS = 4096.0
GAIN_STEPS = 4096.0
REST_STEPS = 2.0**27
COPIES = 1
VMEM_LIMIT = 24 * 1024 * 1024
f32, bf16, i32, i16 = jnp.float32, jnp.bfloat16, jnp.int32, jnp.int16


def basis_rows(channels):
    position = (2.0 * np.arange(channels) + 1.0) / channels - 1.0
    rows = []
    for vector in [np.ones_like(position), position, position**2, position**3]:
        for other in rows:
            vector = vector - np.sum(other * vector) * other
        rows.append(vector / np.sqrt(np.sum(vector * vector)))
    return np.stack(rows).astype(np.float32)


def lanes_of(rows):
    start = 2 * rows + 3 * rows // 4
    return {"re": 0, "im": rows, "misc": 2 * rows, "start": start, "scale": start + LANES}


def rows_of(data_ref):
    return (data_ref.shape[2] - 2 * LANES) * 4 // 11


def coded(values):
    return jnp.round(values).astype(i32).astype(i16)


def pick_channel_pair(by_direction, pair):
    return jnp.concatenate([block[2 * pair : 2 * pair + 2] for block in by_direction], 0)


def pack_kernel(
    coh_hbm, vis_hbm, pairs_hbm, out_ref, coh_ref, vis_ref, pairs_ref, coh_sem, vis_sem, pairs_sem
):
    rows = vis_ref.shape[2]
    count = out_ref.shape[0]
    channels = vis_ref.shape[1]
    at = lanes_of(rows)
    half = rows // 2
    piece = half // COPIES
    pairs_copy = pltpu.make_async_copy(pairs_hbm, pairs_ref, pairs_sem)
    pairs_copy.start()
    copies = []
    for index in range(COPIES):
        group = []
        for side in range(2):
            lanes = pl.ds(side * half + index * piece, piece)
            slot = 2 * index + side
            group.append(
                pltpu.make_async_copy(
                    coh_hbm.at[:, :, :, lanes], coh_ref.at[:, :, :, lanes], coh_sem.at[slot]
                )
            )
            group.append(
                pltpu.make_async_copy(vis_hbm.at[:, :, lanes], vis_ref.at[:, :, lanes], vis_sem.at[slot])
            )
        copies.append(group)
    for kind in (1, 0):
        for group in copies:
            for copy in group[kind::2]:
                copy.start()
    for group in copies:
        for copy in group[1::2]:
            copy.wait()
    peak = jnp.zeros((channels, LANES), f32)
    for start in range(0, rows, LANES):
        for part in range(2):
            peak = jnp.maximum(peak, jnp.abs(vis_ref[part, :, start : start + LANES]))
    peak = jnp.max(peak, axis=(0, 1), keepdims=True)
    exponent = jnp.full((1, 1), -60.0, f32)
    inverse = jnp.full((1, 1), 2.0**60, f32)
    for power in range(-60, -8):
        over = peak > 32767.0 * 2.0**power
        exponent = jnp.where(over, power + 1.0, exponent)
        inverse = jnp.where(over, 2.0 ** (-power - 1), inverse)
    exponent = coded(jnp.broadcast_to(exponent, (8, LANES)))
    for p in range(count):
        out_ref[p, :, at["scale"] : at["scale"] + LANES] = exponent
    pairs_copy.wait()

    def misc(group, carry):
        columns = [pl.ds(pl.multiple_of((4 * group + k) * LANES, LANES), LANES) for k in range(4)]
        stations = coded(jnp.concatenate([pairs_ref[:, lanes].astype(f32) for lanes in columns], 0))
        seen = [[vis_ref[part, :, lanes] * inverse for lanes in columns] for part in range(2)]
        place = at["misc"] + 3 * LANES * group
        places = [pl.ds(pl.multiple_of(place + k * LANES, LANES), LANES) for k in range(3)]
        for p in range(count):
            out_ref[p, :, places[0]] = coded(pick_channel_pair(seen[0], p))
            out_ref[p, :, places[1]] = coded(pick_channel_pair(seen[1], p))
            out_ref[p, :, places[2]] = stations
        return carry

    lax.fori_loop(0, rows // (4 * LANES), misc, 0)

    def columns(index, carry):
        early = pl.multiple_of(index * LANES, LANES)
        late = pl.multiple_of(half + index * LANES, LANES)
        for offset in (early, late):
            lanes = pl.ds(offset, LANES)
            for part in range(2):
                blocks = [coh_ref[part, d, :, lanes].astype(f32) * COH_STEPS for d in range(SKY_DIRECTIONS)]
                place = pl.multiple_of(offset + part * rows, LANES)
                for p in range(count):
                    out_ref[p, :, pl.ds(place, LANES)] = coded(pick_channel_pair(blocks, p))
        return carry

    step = piece // LANES
    for index, group in enumerate(copies):
        for copy in group[0::2]:
            copy.wait()
        lax.fori_loop(index * step, (index + 1) * step, columns, 0)


def seed_kernel(core_ref, mine_ref, other_ref, packed_ref, out_ref, block_ref, block_sem):
    count = block_ref.shape[0]
    is_first = core_ref[0] == 0
    parts = []
    for part in range(2):
        mine = jnp.concatenate([mine_ref[part, d] for d in range(SKY_DIRECTIONS)], 1)
        other = jnp.concatenate([other_ref[part, d] for d in range(SKY_DIRECTIONS)], 1)
        start = jnp.concatenate([jnp.where(is_first, mine, other), jnp.where(is_first, other, mine)], 0)
        coarse = jnp.round(start * GAIN_STEPS)
        parts += [coarse, jnp.round((start - coarse * (1.0 / GAIN_STEPS)) * REST_STEPS)]
    square = jnp.concatenate(parts, 0).T
    blocks = [square[d * 2 * count : (d + 1) * 2 * count] for d in range(SKY_DIRECTIONS)]
    for p in range(count):
        block_ref[p] = coded(pick_channel_pair(blocks, p))
    width = out_ref.shape[2]
    copy = pltpu.make_async_copy(block_ref, out_ref.at[:, :, width - 2 * LANES : width - LANES], block_sem)
    copy.start()
    copy.wait()


def stations_in_lanes(pieces):
    lane = lax.broadcasted_iota(i32, (8, LANES), 1)
    tiles = []
    for q in range(0, len(pieces), 4):
        tile = pieces[q]
        for k in range(1, 4):
            moved = pltpu.roll(pieces[q + k], 32 * k, 1)
            tile = jnp.where(lane >= 32 * k, moved, tile)
        tiles.append(tile)
    return jnp.concatenate(tiles, 1)


def starting_gains(data_ref):
    at = lanes_of(rows_of(data_ref))["start"]
    parts = []
    for part in range(2):
        pieces = []
        for p in range(data_ref.shape[0]):
            piece = data_ref[p, :, at : at + LANES].astype(i32).astype(f32)
            if part:
                piece = pltpu.roll(piece, LANES - 64, 1)
            piece = piece * (1.0 / GAIN_STEPS) + pltpu.roll(piece, LANES - 32, 1) * (1.0 / REST_STEPS)
            pieces.append(piece)
        parts.append(stations_in_lanes(pieces))
    return parts


def lookup(words, low, high):
    picked = [jnp.take_along_axis(w, low, axis=1, mode="promise_in_bounds") for w in words]
    odd, upper = (high & 1) == 1, (high & 2) == 2
    word = jnp.where(
        upper, jnp.where(odd, picked[3], picked[2]), jnp.where(odd, picked[1], picked[0])
    )
    return (word >> 16).astype(f32), ((word & 65535) - 32768).astype(f32)


def words_of(gains_re, gains_im):
    rounded_re = gains_re.astype(bf16).astype(f32)
    rounded_im = gains_im.astype(bf16).astype(f32)
    peak = jnp.max(jnp.maximum(jnp.abs(rounded_re), jnp.abs(rounded_im)), axis=(0, 1), keepdims=True)
    unit = jnp.full((1, 1), 2.0**-60, f32)
    for power in range(-60, 60):
        unit = jnp.where(peak > 32767.0 * 2.0**power, 2.0 ** (power + 1), unit)
    inverse = 1.0 / unit
    scaled_re = jnp.round(rounded_re * inverse).astype(i32)
    scaled_im = jnp.round(rounded_im * inverse).astype(i32)
    word = (scaled_re << 16) + (scaled_im + 32768)
    return [word[:, h * LANES : (h + 1) * LANES] for h in range(PARTS)], unit


def column_terms(coh_re, coh_im, seen_re, seen_im, stations, place, words, square, sublane):
    def station(row):
        index = jnp.broadcast_to(stations[row : row + 1], (8, LANES))
        return index & (LANES - 1), index >> 7

    low_first, high_first = station(2 * place)
    low_second, high_second = station(2 * place + 1)
    near_re, near_im = lookup(words, low_first, high_first)
    far_re, far_im = lookup(words, low_second, high_second)
    z_re = coh_re * far_re + coh_im * far_im
    z_im = coh_im * far_re - coh_re * far_im
    x_re = near_re * coh_re - near_im * coh_im
    x_im = near_re * coh_im + near_im * coh_re
    inside = (sublane >> 1) == place
    vis_re = jnp.where(inside, seen_re, 0.0)
    vis_im = jnp.where(inside, seen_im, 0.0)
    res_re = vis_re - square * (near_re * z_re - near_im * z_im)
    res_im = vis_im - square * (near_re * z_im + near_im * z_re)
    res_re = res_re + pltpu.roll(res_re, 4, 0)
    res_re = res_re + pltpu.roll(res_re, 2, 0)
    res_im = res_im + pltpu.roll(res_im, 4, 0)
    res_im = res_im + pltpu.roll(res_im, 2, 0)
    first = jnp.concatenate([res_re * z_re + res_im * z_im, res_im * z_re - res_re * z_im], 0)
    second = jnp.concatenate([res_re * x_re + res_im * x_im, res_re * x_im - res_im * x_re], 0)
    first_norm = z_re * z_re + z_im * z_im
    second_norm = x_re * x_re + x_im * x_im
    twice = lambda a: jnp.concatenate([a, a], 0).astype(bf16)
    return (
        (first.astype(bf16), twice(first_norm), low_first, high_first),
        (second.astype(bf16), twice(second_norm), low_second, high_second),
    )


def operands(term, station_rows, half_rows):
    pair, norm, low, high = term
    zero = jnp.zeros_like(pair)
    high = jnp.broadcast_to(high[:1], (16, LANES)).astype(i16)
    rows = [jnp.where(high == i16(h), pair, zero) for h in range(PARTS)]
    rows += [jnp.where(high == half_rows + i16(h), norm, zero) for h in range(0, PARTS, 2)]
    low = jnp.broadcast_to(low[:1].astype(f32), (LANES, LANES)).astype(bf16)
    table = jnp.where(station_rows == low, jnp.ones_like(low), jnp.zeros_like(low))
    return jnp.concatenate(rows, 0), table


def accumulate(data_ref, first, count, gains_re, gains_im, sums_ref, acc_ref, before=None):
    rows = rows_of(data_ref)
    at = lanes_of(rows)
    words, unit = words_of(gains_re, gains_im)
    square = jnp.broadcast_to(unit * unit * (1.0 / COH_STEPS), (8, LANES))
    unit = unit * (1.0 / COH_STEPS)
    station_rows = lax.broadcasted_iota(i32, (LANES, LANES), 0).astype(f32).astype(bf16)
    half_rows = (lax.broadcasted_iota(i32, (16, LANES), 0) >> 3).astype(i16)
    sublane = lax.broadcasted_iota(i32, (8, LANES), 0)
    acc_ref[...] = jnp.zeros_like(acc_ref)

    def step(source, carry):
        left, right = [], []
        load = lambda start: data_ref[source, :, start : start + LANES].astype(i32)
        vis_unit = jnp.exp2(load(at["scale"]).astype(f32))
        for offset in range(0, rows, LANES):
            place = offset // LANES % 4
            if place == 0:
                group = at["misc"] + 3 * offset // 4
                seen_re = load(group).astype(f32) * vis_unit
                seen_im = load(group + LANES).astype(f32) * vis_unit
                stations = load(group + 2 * LANES)
            terms = column_terms(
                load(at["re"] + offset).astype(f32),
                load(at["im"] + offset).astype(f32),
                seen_re,
                seen_im,
                stations,
                place,
                words,
                square,
                sublane,
            )
            (rows_first, table_first), (rows_second, table_second) = [
                operands(term, station_rows, half_rows) for term in terms
            ]
            left.append(jnp.concatenate([rows_first, rows_second], 0))
            right.append(jnp.concatenate([table_first, table_second], 0))
        acc_ref[...] += lax.dot_general(
            jnp.concatenate(right, 1),
            jnp.concatenate(left, 1),
            (((1,), (1,)), ((), ())),
            preferred_element_type=f32,
        )
        return carry

    lax.fori_loop(first, first + count, step, 0, unroll=UNROLL)
    tall = 24 * PARTS
    acc = (acc_ref[0:LANES, 0:tall] + acc_ref[LANES : 2 * LANES, tall : 2 * tall]).T
    base = 16 * PARTS
    sums = [
        jnp.concatenate([acc[16 * h : 16 * h + 8] for h in range(PARTS)], 1),
        jnp.concatenate([acc[16 * h + 8 : 16 * h + 16] for h in range(PARTS)], 1),
        jnp.concatenate([acc[base + 8 * h : base + 8 * h + 8] for h in range(PARTS)], 1),
    ]
    for k, factor in enumerate((unit, unit, unit * unit)):
        part = sums[k] * factor
        sums_ref[k] = part if before is None else before[k] + part


def advance(gains, sums, target, penalty_weight):
    return gains + (sums[0:2] + penalty_weight * (target - gains)) / (
        2.0 * sums[2] + penalty_weight
    )


def first_kernel(data_ref, sums_ref, gains_ref, acc_ref):
    gains = starting_gains(data_ref)
    gains_ref[0], gains_ref[1] = gains
    accumulate(data_ref, 0, data_ref.shape[0], *gains, sums_ref, acc_ref)


def early_kernel(data_ref, gains_ref, sums_ref, acc_ref):
    accumulate(data_ref, 0, data_ref.shape[0] // 2, gains_ref[0], gains_ref[1], sums_ref, acc_ref)


def late_kernel(data_ref, gains_ref, before_ref, sums_ref, acc_ref):
    half = data_ref.shape[0] // 2
    accumulate(data_ref, half, half, gains_ref[0], gains_ref[1], sums_ref, acc_ref, before_ref)


def step_kernel(weight, data_ref, mine_ref, other_ref, gains_ref, sums_ref, new_ref, acc_ref):
    gains = gains_ref[...]
    gains = advance(gains, mine_ref[...] + other_ref[...], gains, weight)
    new_ref[...] = gains
    accumulate(data_ref, 0, data_ref.shape[0], gains[0], gains[1], sums_ref, acc_ref)


def retarget_kernel(
    weight, data_ref, mine_ref, other_ref, gains_ref, fit_ref, sums_ref, new_ref, target_ref, acc_ref
):
    consensus = by_channel(fit_ref)
    gains = gains_ref[...]
    target = consensus - (gains - consensus)
    target_ref[...] = target
    gains = advance(gains, mine_ref[...] + other_ref[...], target, weight)
    new_ref[...] = gains
    accumulate(data_ref, 0, data_ref.shape[0], gains[0], gains[1], sums_ref, acc_ref)


def by_channel(block_ref):
    pieces = [block_ref[p] for p in range(block_ref.shape[0])]
    turned = [pltpu.roll(piece, LANES - 32, 1) for piece in pieces]
    return jnp.stack([stations_in_lanes(pieces), stations_in_lanes(turned)])


def finish_kernel(weight, mine_ref, other_ref, gains_ref, target_ref, new_ref, block_ref):
    gains = advance(gains_ref[...], mine_ref[...] + other_ref[...], target_ref[...], weight)
    new_ref[...] = gains
    lane = lax.broadcasted_iota(i32, (8, LANES), 1)
    for p in range(block_ref.shape[0]):
        tile = slice(p // 4 * LANES, (p // 4 + 1) * LANES)
        shift = 32 * (p % 4)
        real = pltpu.roll(gains[0][:, tile], (LANES - shift) % LANES, 1)
        imag = pltpu.roll(gains[1][:, tile], (LANES + 32 - shift) % LANES, 1)
        block_ref[p] = jnp.where(lane < 32, real, imag)


def is_even(shape):
    return (lax.broadcasted_iota(i32, shape, 0) & 1) == 0


def basis_column(basis_ref, row, source):
    return basis_ref[row, source]


def fit_kernel(basis_ref, *refs):
    *block_refs, out_ref = refs
    even = is_even((8, LANES))
    blocks = []
    for p in range(block_refs[0].shape[0]):
        blend = block_refs[0][p]
        if len(block_refs) > 1:
            blend = blend + block_refs[1][p]
        blocks.append(blend)
    totals = []
    for row in range(4):
        total = sum(basis_column(basis_ref, row, p) * block for p, block in enumerate(blocks))
        totals.append(total + jnp.where(even, pltpu.roll(total, 7, 0), pltpu.roll(total, 1, 0)))
    lane = lax.broadcasted_iota(i32, (8, LANES), 1)
    early = jnp.where(even, totals[0], totals[1])
    late = jnp.where(even, totals[2], totals[3])
    packed = jnp.where(lane < LANES // 2, early, pltpu.roll(late, LANES // 2, 1))
    for f in range(out_ref.shape[0]):
        out_ref[f] = packed


def consensus_blocks(basis_ref, parts_ref, count):
    even = is_even((8, LANES))
    total = parts_ref[0]
    for f in range(1, parts_ref.shape[0]):
        total = total + parts_ref[f]
    rows = []
    for half in (total, pltpu.roll(total, LANES // 2, 1)):
        rows.append(jnp.where(even, half, pltpu.roll(half, 1, 0)))
        rows.append(jnp.where(even, pltpu.roll(half, 7, 0), half))
    return [
        sum(basis_column(basis_ref, row, p) * rows[row] for row in range(4)) for p in range(count)
    ]


def spread_kernel(basis_ref, parts_ref, gains_ref, out_ref, dual_ref):
    for p, block in enumerate(consensus_blocks(basis_ref, parts_ref, out_ref.shape[0])):
        out_ref[p] = block
        dual_ref[p] = gains_ref[p] - block


def write_owned(blocks, is_first, out_ref):
    owned = out_ref.shape[2]
    channels = 2 * len(blocks)
    rows = [block[2 * d : 2 * d + 2] for d in range(SKY_DIRECTIONS) for block in blocks]
    turned = jnp.concatenate(rows, 0).T
    for part in range(2):
        both = turned[part * 2 * owned : (part + 1) * 2 * owned]
        mine = jnp.where(is_first, both[:owned], both[owned:])
        for d in range(SKY_DIRECTIONS):
            out_ref[part, d] = mine[:, d * channels : (d + 1) * channels]


def place_kernel(core_ref, blocks_ref, out_ref):
    write_owned([blocks_ref[p] for p in range(blocks_ref.shape[0])], core_ref[0] == 0, out_ref)


def final_kernel(core_ref, basis_ref, parts_ref, out_ref):
    count = out_ref.shape[3] // 2
    write_owned(consensus_blocks(basis_ref, parts_ref, count), core_ref[0] == 0, out_ref)


def call(
    name,
    kernel,
    out_shape,
    *inputs,
    scalars=0,
    outside=(),
    aliases=None,
    flops=0,
    scratch=(),
):
    whole = pl.BlockSpec(memory_space=pltpu.VMEM)
    anywhere = pl.BlockSpec(memory_space=pl.ANY)
    specs = [pl.BlockSpec(memory_space=pltpu.SMEM)] * scalars
    specs += [anywhere if k in outside else whole for k in range(scalars, len(inputs))]
    return pl.pallas_call(
        kernel,
        out_shape=out_shape,
        in_specs=specs,
        out_specs=jax.tree.map(lambda _: anywhere if aliases else whole, out_shape),
        scratch_shapes=list(scratch),
        input_output_aliases=aliases or {},
        compiler_params=pltpu.CompilerParams(vmem_limit_bytes=VMEM_LIMIT),
        cost_estimate=pl.CostEstimate(
            flops=flops, bytes_accessed=sum(x.size * x.dtype.itemsize for x in inputs), transcendentals=0
        ),
        name=name,
    )(*inputs)


def shards(vis, coherency, gains_init, station_pairs):
    channels_dev = vis.shape[1]
    rows_dev = vis.shape[2]
    owned = gains_init.shape[3]
    pairs = lax.axis_size("pair")
    bands = lax.axis_size("freq")
    assert channels_dev == 2 * pairs and owned == 16 and STATION_TOTAL == 2 * owned * pairs
    assert ROUNDS == 2 and ITERS == 2
    weight = 2.0 * rows_dev * pairs * 2 / STATION_TOTAL
    swap = [(0, 1), (1, 0)]
    core = lax.axis_index("core").astype(i32).reshape(1)
    basis = lax.dynamic_slice_in_dim(
        jnp.asarray(basis_rows(channels_dev * bands)),
        lax.axis_index("freq") * channels_dev,
        channels_dev,
        1,
    )
    basis = basis.reshape(4, pairs, 1, 2, 1)
    basis = jnp.broadcast_to(basis, (4, pairs, SKY_DIRECTIONS, 2, LANES)).reshape(4, pairs, 8, LANES)
    shape = jax.ShapeDtypeStruct
    gains_shape = shape((2, 8, STATION_TOTAL), f32)
    sums_shape = shape((3, 8, STATION_TOTAL), f32)
    block_shape = shape((pairs, 8, LANES), f32)
    parts_shape = shape((bands, 8, LANES), f32)
    out_shape = shape((2, SKY_DIRECTIONS, owned, channels_dev), f32)
    width = 11 * rows_dev // 4 + 2 * LANES
    flops = 2 * rows_dev * pairs * 192 * 256
    scratch = [pltpu.VMEM((2 * LANES, 48 * PARTS), f32)]
    sweep = functools.partial(call, flops=flops, scratch=scratch)
    half_sweep = functools.partial(call, flops=flops // 2, scratch=scratch)

    def in_hbm(array):
        return pltpu.with_memory_space_constraint(array, pltpu.HBM)

    def exchange(partial):
        return lax.ppermute(partial, "core", swap)

    def to_pairs(block):
        return lax.all_to_all(block, "pair", 0, 0, tiled=True)

    def over_bands(block):
        return lax.all_to_all(block, "freq", 0, 0, tiled=True)

    start = gains_init.transpose(0, 1, 3, 2)
    packed_shape = shape((pairs, 8, width), i16)
    packed = call(
        "pack",
        pack_kernel,
        packed_shape,
        in_hbm(coherency),
        in_hbm(vis),
        in_hbm(station_pairs),
        outside=(0, 1, 2),
        scratch=[
            pltpu.VMEM(coherency.shape, bf16),
            pltpu.VMEM(vis.shape, f32),
            pltpu.VMEM(station_pairs.shape, i32),
            pltpu.SemaphoreType.DMA((2 * COPIES,)),
            pltpu.SemaphoreType.DMA((2 * COPIES,)),
            pltpu.SemaphoreType.DMA,
        ],
    )
    packed = call(
        "seed",
        seed_kernel,
        packed_shape,
        core,
        start,
        exchange(start),
        packed,
        scalars=1,
        outside=(3,),
        aliases={3: 0},
        scratch=[pltpu.VMEM((pairs, 8, LANES), i16), pltpu.SemaphoreType.DMA],
    )
    data = to_pairs(packed)

    sums, gains = sweep("first", first_kernel, (sums_shape, gains_shape), data)
    target = gains
    sums, gains = sweep(
        "step",
        functools.partial(step_kernel, weight),
        (sums_shape, gains_shape),
        data,
        sums,
        exchange(sums),
        gains,
    )
    finish = functools.partial(finish_kernel, weight)
    gains, block = call("finish", finish, (gains_shape, block_shape), sums, exchange(sums), gains, target)
    owner_gains = to_pairs(block)
    sums = half_sweep("early", early_kernel, sums_shape, data, gains)
    owner_gains, sums = lax.optimization_barrier((owner_gains, sums))
    parts = over_bands(call("fit", fit_kernel, parts_shape, basis, owner_gains))
    sums = half_sweep("late", late_kernel, sums_shape, data, gains, sums)
    parts, sums = lax.optimization_barrier((parts, sums))
    block, owner_dual = call(
        "spread", spread_kernel, (block_shape, block_shape), basis, parts, owner_gains
    )
    fit = to_pairs(block)

    sums, gains, target = sweep(
        "retarget",
        functools.partial(retarget_kernel, weight),
        (sums_shape, gains_shape, gains_shape),
        data,
        sums,
        exchange(sums),
        gains,
        fit,
    )
    gains, block = call("finish", finish, (gains_shape, block_shape), sums, exchange(sums), gains, target)
    owner_gains = to_pairs(block)
    parts = over_bands(call("fit", fit_kernel, parts_shape, basis, owner_gains, owner_dual))
    final_gains = call("place", place_kernel, out_shape, core, owner_gains, scalars=1)
    final_consensus = call("final", final_kernel, out_shape, core, basis, parts, scalars=1)
    return (final_gains.transpose(0, 1, 3, 2), final_consensus.transpose(0, 1, 3, 2))


def solution(mesh):
    split = Mesh(
        mesh.devices.reshape(mesh.shape["freq"], mesh.shape["bl"] // 2, 2), ("freq", "pair", "core")
    )
    bl = ("pair", "core")
    placed = (
        P(None, "freq", bl),
        P(None, None, "freq", bl),
        P(None, None, "freq", bl),
        P(None, bl),
    )
    return jax.shard_map(
        shards,
        mesh=split,
        in_specs=placed,
        out_specs=(P(None, None, "freq", bl), P(None, None, "freq", bl)),
        check_vma=False,
    )
```
